32 devices in a mesh: groups: 2 (over x), space: 8 (over z, y), chan: 2 (over core).
Axes of the slice: x: 2, y: 2, z: 4, core: 2. Of those that a mesh axis runs over, the one named last changes fastest.
Arguments:
- inputs: float32 [128, 32, 2, 256], P('chan', ('groups', 'space')), parts along dimension 1, may hold values from -6 to 6
- weights: float32 [128, 27, 128], replicated, may hold values from -0.109375 to 0.109375
- out_grad: float32 [128, 32, 2, 256], P('chan', ('groups', 'space')), parts along dimension 1, may hold values from -6 to 6
Outputs:
- outputs: float32 [128, 32, 2, 256], P('chan', ('groups', 'space')), parts along dimension 1
- in_grad: float32 [128, 32, 2, 256], P('chan', ('groups', 'space')), parts along dimension 1
- filter_grad: float32 [128, 54, 128], P('chan', 'groups'), parts along dimension 1
The draws below stay inside these ranges and needn't reach their ends.
There are 2 independent parts, one for each index of `groups`. The reference program is written for one: setup_inputs(seed, part) draws one part's arguments, and reference() takes and returns one part's arrays. A program takes and returns all parts, laid end to end along the dimension named above; an argument that names none is the same for every part. Nothing has to cross between parts.
All inputs are finite; a program needn't handle non-finite values.
Results may differ from the reference program's by a relative error of at most 0.0001.
Values sent between devices are 32-bit elements; how exact they have to be, the bound alone decides.
No kernel may reach another device: no remote copies, remote signals or barrier semaphores. Data moves between devices by JAX's collectives and lax.ppermute only.
A program may use at most 128 MiB of HBM per device.

```python
import jax
import jax.numpy as jnp
from jax import lax

C = 128
ZW = 2
NY = 256
NX = 16


def steps_of(stream_key, dims, pieces, smallest, top_value):
    def one(axis_at, blocks):
        heights = jax.random.uniform(jax.random.fold_in(jax.random.fold_in(stream_key, 6), axis_at), (blocks,), jnp.float32, smallest / len(pieces), top_value / len(pieces))
        return jnp.repeat(jnp.exp(heights), dims[axis_at] // blocks).reshape((-1,) + (1,) * (len(dims) - axis_at - 1))

    gain = one(*pieces[0])
    for cut in pieces[1:]:
        gain = gain * one(*cut)
    return gain


def bell_draw(own_key, extent, deviation, limit, split=(), held_as=jnp.bfloat16):
    result = jax.random.normal(own_key, extent, jnp.float32) * deviation
    if len(split) > 0:
        result = steps_of(own_key, extent, split, -0.22, 0.18) * result
    return jnp.clip(result, min=-limit, max=limit).astype(held_as)


def setup_inputs(seed: int = 0, part: int = 0) -> dict:
    key_of = jax.random.split(jax.random.key(seed), 4)
    own_keys = jax.random.split(jax.random.fold_in(key_of[3], part), 4)
    return {
        "inputs": bell_draw(own_keys[0], (C, NX, ZW, NY), 1.0, 6.0, ((0, 2), (1, 8)), jnp.float32),
        "weights": bell_draw(key_of[1], (C, 27, C), (27 * C) ** -0.5, 0.109375, (), jnp.float32),
        "out_grad": bell_draw(own_keys[2], (C, NX, ZW, NY), 1.0, 6.0, ((0, 2), (1, 8)), jnp.float32),
    }


HIGH = lax.Precision.HIGHEST

def padded(field):
    return jnp.pad(field, ((0, 0), (1, 1), (1, 1), (1, 1)))

def window(source, first, second, third, shape):
    return source[:, first:first + shape[1], second:second + shape[2], third:third + shape[3]]

def reference(inputs, weights, out_grad):
    shape = inputs.shape
    input_pad = padded(inputs)
    grad_pad = padded(out_grad)
    outputs = jnp.zeros(shape, jnp.float32)
    in_grad = jnp.zeros(shape, jnp.float32)
    taps = []
    for first in range(3):
        for second in range(3):
            for third in range(3):
                offset = 9 * first + 3 * second + third
                tap = weights[:, offset, :]
                forward_win = window(input_pad, first, second, third, shape)
                back_win = window(grad_pad, 2 - first, 2 - second, 2 - third, shape)
                outputs = outputs + jnp.einsum('oi,ixzy->oxzy', tap, forward_win, precision=HIGH)
                in_grad = in_grad + jnp.einsum('oi,oxzy->ixzy', tap, back_win, precision=HIGH)
                taps.append(jnp.einsum('oxzy,ixzy->oi', out_grad, forward_win, precision=HIGH))
    scale = 1.0 / jnp.sqrt(jnp.float32(shape[1] * shape[2] * shape[3]))
    filter_grad = jnp.stack(taps, axis=1) * scale
    return (outputs, in_grad, filter_grad)
```

```python
import jax
import jax.numpy as jnp
from jax import lax
from jax.experimental import pallas as pl
from jax.experimental.pallas import tpu as pltpu
from jax.sharding import PartitionSpec as P

F32 = jnp.float32
BF16 = jnp.bfloat16
VMEM = pl.BlockSpec(memory_space=pltpu.VMEM)
SMEM = pl.BlockSpec(memory_space=pltpu.SMEM)
NN = (((1,), (0,)), ((), ()))
NT = (((1,), (1,)), ((), ()))


def call(body, out_shape, n_in, scratch=()):
    return pl.pallas_call(
        body,
        out_shape=out_shape,
        in_specs=[SMEM] + [VMEM] * n_in,
        out_specs=jax.tree.map(lambda _: VMEM, out_shape),
        scratch_shapes=scratch,
        compiler_params=pltpu.CompilerParams(vmem_limit_bytes=40 << 20),
    )


def halves(value):
    high = value.astype(BF16)
    return high, (value - high.astype(F32)).astype(BF16)


def dot3(a_hi, a_lo, b_hi, b_lo, dims):
    def dot(a, b):
        return lax.dot_general(a, b, dims, preferred_element_type=F32)

    return dot(a_hi, b_hi) + (dot(a_hi, b_lo) + dot(a_lo, b_hi))


def moved(value, step):
    width = value.shape[-1]
    lane = lax.broadcasted_iota(jnp.int32, value.shape, value.ndim - 1)
    edge = 0 if step > 0 else width - 1
    return jnp.where(lane == edge, 0.0, pltpu.roll(value, step % width, value.ndim - 1))


def weight_kernel(at, w, a_hi, a_lo, b_hi, b_lo, turned):
    side, chan = at[1], at[2]
    sign = 1 - 2 * side
    half = a_hi.shape[1] // 6
    full = 2 * half
    own = pl.ds(pl.multiple_of(chan * half, half), half)
    for first in range(3):
        for second in range(3):
            for third in range(3):
                tap = 9 * first + 3 * second + third
                turned[...] = w[tap].T
                fwd = halves(w[tap, own, :])
                back = halves(turned[own, :])
                fwd_at = 1 + (first - 1) * sign
                back_at = 1 - (first - 1) * sign
                for low in range(2):
                    up = low + second - 1
                    if up < 0 or up > 1:
                        continue
                    row = (low * 3 + third) * half
                    a_hi[fwd_at, row : row + half, up * full : up * full + full] = fwd[0]
                    a_lo[fwd_at, row : row + half, up * full : up * full + full] = fwd[1]
                    row = (up * 3 + 2 - third) * half
                    b_hi[back_at, row : row + half, low * full : low * full + full] = back[0]
                    b_lo[back_at, row : row + half, low * full : low * full + full] = back[1]


def put_slab(hi, lo, chan, own, other):
    half = own.shape[1]
    for z in range(2):
        for piece, place in ((own, chan), (other, 1 - chan)):
            rows = pl.ds(pl.multiple_of((2 * z + place) * half, half), half)
            hi[rows, :], lo[rows, :] = halves(piece[z])


def conv_kernel(at, halo, halo2, own, own2, pair, pair2, w_hi, w_lo, out, x_hi, x_lo):
    side, chan = at[1], at[2]
    half = own.shape[2]
    put_slab(x_hi.at[0], x_lo.at[0], chan, halo, halo2)
    put_slab(x_hi.at[1], x_lo.at[1], chan, own.at[side], own2.at[side])
    put_slab(x_hi.at[2], x_lo.at[2], chan, own.at[1 - side], own2.at[1 - side])
    put_slab(x_hi.at[3], x_lo.at[3], chan, pair.at[side], pair2.at[side])
    for t in range(2):
        total = jnp.zeros((6 * half, own.shape[3]), F32)
        for d in range(3):
            total = total + dot3(w_hi[d], w_lo[d], x_hi[t + d], x_lo[t + d], NN)
        slab = side if t == 0 else 1 - side
        for z in range(2):
            low, mid, high = (
                total[(3 * z + c) * half : (3 * z + c + 1) * half, :] for c in range(3)
            )
            out[slab, z] = mid + moved(low, 1) + moved(high, -1)


def filter_kernel(at, own, own2, pair, pair2, edge, edge2, g_own, g_pair, *rest):
    count = len(rest) - 7
    outs = rest[:count]
    x_hi, x_lo, g_hi, g_lo, acc1, acc0, flat = rest[count:]
    z_at, side, chan = at[0], at[1], at[2]
    half = own.shape[2]
    part = half // 2
    slabs = (
        (own.at[side], own2.at[side]),
        (own.at[1 - side], own2.at[1 - side]),
        (pair.at[side], pair2.at[side]),
        (pair.at[1 - side], pair2.at[1 - side]),
        (edge, edge2),
    )
    grads = (g_own.at[side], g_own.at[1 - side], g_pair.at[side], g_pair.at[1 - side])
    for t in range(5):
        put_slab(x_hi.at[t], x_lo.at[t], chan, *slabs[t])
    for t in range(4):
        for z in range(2):
            value = grads[t][z]
            for c, shifted in enumerate((moved(value, -1), value, moved(value, 1))):
                row = (3 * z + c) * half
                g_hi[t, row : row + half, :], g_lo[t, row : row + half, :] = halves(shifted)
    total = None
    for t in range(4):
        term = dot3(g_hi[t], g_lo[t], x_hi[t + 1], x_lo[t + 1], NT)
        total = term if total is None else total + term
    acc1[...] = total

    def some(ref, t):
        pieces = [
            ref[t, pl.ds(pl.multiple_of(k * half + side * part, part), part), :] for k in range(6)
        ]
        return jnp.concatenate(pieces, axis=0)

    total = None
    for t in range(4):
        term = dot3(some(g_hi, t), some(g_lo, t), x_hi[t], x_lo[t], NT)
        total = term if total is None else total + term
    acc0[...] = total

    tiles = flat.shape[0]
    place = 0
    for acc, size in ((acc1, half), (acc0, part)):
        full = 2 * half
        for b in range(3):
            for c in range(3):
                lower = acc[c * size : (c + 1) * size, :]
                upper = acc[(3 + c) * size : (4 + c) * size, :]
                if b == 0:
                    value = upper[:, :full]
                elif b == 1:
                    value = lower[:, :full] + upper[:, full:]
                else:
                    value = lower[:, full:]
                flat[place : place + size // 8] = value.reshape(size // 8, 8, full)
                place += size // 8
    if place < tiles:
        flat[place:] = jnp.zeros((tiles - place, 8, 2 * half), F32)
    each = tiles // count
    for k in range(count):
        outs[k][...] = flat[pl.ds(lax.rem(z_at + k, count) * each, each)]


def sum_kernel(scale, at, *refs):
    total = refs[0][...]
    for ref in refs[1:-1]:
        total = total + ref[...]
    refs[-1][...] = total * scale


def join_kernel(at, *refs):
    count = (len(refs) - 3) // 2
    mine, theirs = refs[:count], refs[count : 2 * count]
    out, flat, flat2 = refs[2 * count :]
    z_at, side = at[0], at[1]
    each = mine[0].shape[0]
    for k in range(count):
        here = pl.ds(lax.rem(z_at + count - k, count) * each, each)
        flat[here] = mine[k][...]
        flat2[here] = theirs[k][...]
    rows = out.shape[1]
    for source, which in ((flat, side), (flat2, 1 - side)):
        first = source[: 9 * rows].reshape(9, rows, 8, out.shape[3])
        out[pl.ds((1 - which) * 18, 9)] = first
        rest = source[9 * rows : 9 * rows + 9 * rows // 2]
        out[9:18, pl.ds(which * (rows // 2), rows // 2)] = rest.reshape(
            9, rows // 2, 8, out.shape[3]
        )


def local(inputs, weights, out_grad):
    half, _, _, width = inputs.shape
    full = 2 * half
    ring = lax.axis_size("space")
    count = ring // 2
    here = lax.axis_index("space")
    z_at, side, chan = here // 2, here % 2, lax.axis_index("chan")
    at = jnp.stack([z_at, side, chan]).astype(jnp.int32)

    def swap_chan(value):
        return lax.ppermute(value, "chan", [(0, 1), (1, 0)])

    def swap_side(value):
        return lax.ppermute(value, "space", [(i, i ^ 1) for i in range(ring)])

    def shift(value, step):
        pairs = [(2 * z + y, 2 * ((z + step) % count) + y) for z in range(count) for y in range(2)]
        return lax.ppermute(value, "space", pairs)

    def outward(value):
        pairs = []
        for z in range(count):
            if z > 0:
                pairs.append((2 * z, 2 * z - 2))
            if z + 1 < count:
                pairs.append((2 * z + 1, 2 * z + 3))
        return lax.ppermute(value, "space", pairs)

    x_own = inputs.transpose(1, 2, 0, 3)
    x_pair = swap_side(x_own)
    g_own = out_grad.transpose(1, 2, 0, 3)
    g_pair = swap_side(g_own)
    x_edge = outward(lax.dynamic_index_in_dim(x_own, side, 0, keepdims=False))
    g_edge = outward(lax.dynamic_index_in_dim(g_own, side, 0, keepdims=False))
    x_own2 = swap_chan(x_own)
    x_pair2 = swap_chan(x_pair)
    x_edge2 = swap_chan(x_edge)

    w_taps = weights.transpose(1, 0, 2)
    block = jax.ShapeDtypeStruct((3, 6 * half, 2 * full), BF16)
    a_hi, a_lo, b_hi, b_lo = call(
        weight_kernel, [block] * 4, 1, [pltpu.VMEM((full, full), F32)]
    )(at, w_taps)

    tiles = 9 * (half + half // 2) // 8
    each = -(-tiles // count)
    chunk = jax.ShapeDtypeStruct((each, 8, full), F32)
    parts = call(
        filter_kernel,
        [chunk] * count,
        8,
        [
            pltpu.VMEM((5, 2 * full, width), BF16),
            pltpu.VMEM((5, 2 * full, width), BF16),
            pltpu.VMEM((4, 6 * half, width), BF16),
            pltpu.VMEM((4, 6 * half, width), BF16),
            pltpu.VMEM((6 * half, 2 * full), F32),
            pltpu.VMEM((3 * half, 2 * full), F32),
            pltpu.VMEM((each * count, 8, full), F32),
        ],
    )(at, x_own, x_own2, x_pair, x_pair2, x_edge, x_edge2, g_own, g_pair)

    got = [parts[0]] + [shift(parts[k], k) for k in range(1, count)]

    x_halo = swap_side(x_edge)
    g_halo = swap_side(g_edge)
    x_halo2 = swap_chan(x_halo)
    g_halo2 = swap_chan(g_halo)
    g_own2 = swap_chan(g_own)
    g_pair2 = swap_chan(g_pair)
    conv = call(
        conv_kernel,
        jax.ShapeDtypeStruct((2, 2, half, width), F32),
        8,
        [pltpu.VMEM((4, 2 * full, width), BF16)] * 2,
    )
    outputs = conv(at, x_halo, x_halo2, x_own, x_own2, x_pair, x_pair2, a_hi, a_lo)
    in_grad = conv(at, g_halo, g_halo2, g_own, g_own2, g_pair, g_pair2, b_hi, b_lo)

    cells = inputs.shape[1] * ring * inputs.shape[2] * width
    scale = float(1.0 / cells**0.5)
    shard = call(lambda *refs: sum_kernel(scale, *refs), chunk, count)(at, *got)
    mine = [shard] + [shift(shard, k) for k in range(1, count)]
    theirs = [swap_side(value) for value in mine]
    joined = call(
        join_kernel,
        jax.ShapeDtypeStruct((27, half // 8, 8, full), F32),
        2 * count,
        [pltpu.VMEM((each * count, 8, full), F32)] * 2,
    )(at, *mine, *theirs)
    filter_grad = joined.reshape(27, half, full).transpose(1, 0, 2)
    return (
        outputs.transpose(2, 0, 1, 3),
        in_grad.transpose(2, 0, 1, 3),
        filter_grad,
    )


def solution(mesh):
    in_specs = (
        P("chan", ("groups", "space"), None, None),
        P(),
        P("chan", ("groups", "space"), None, None),
    )
    out_specs = (
        P("chan", ("groups", "space"), None, None),
        P("chan", ("groups", "space"), None, None),
        P("chan", "groups", None),
    )
    return jax.shard_map(local, mesh=mesh, in_specs=in_specs, out_specs=out_specs, check_vma=False)
```

```python
import jax
import jax.numpy as jnp
from jax import lax
from jax.experimental import pallas as pl
from jax.experimental.pallas import tpu as pltpu
from jax.sharding import PartitionSpec as P

F32 = jnp.float32
BF16 = jnp.bfloat16
VMEM = pl.BlockSpec(memory_space=pltpu.VMEM)
SMEM = pl.BlockSpec(memory_space=pltpu.SMEM)
NN = (((1,), (0,)), ((), ()))
NT = (((1,), (1,)), ((), ()))


def call(body, out_shape, n_in, scratch=(), cost=None):
    return pl.pallas_call(
        body,
        out_shape=out_shape,
        in_specs=[SMEM] + [VMEM] * n_in,
        out_specs=jax.tree.map(lambda _: VMEM, out_shape),
        scratch_shapes=scratch,
        cost_estimate=cost,
        compiler_params=pltpu.CompilerParams(vmem_limit_bytes=40 << 20),
    )


def halves(value):
    high = value.astype(BF16)
    return high, (value - high.astype(F32)).astype(BF16)


def dot3(a_hi, a_lo, b_hi, b_lo, dims):
    def dot(a, b):
        return lax.dot_general(a, b, dims, preferred_element_type=F32)

    return dot(a_hi, b_hi) + (dot(a_hi, b_lo) + dot(a_lo, b_hi))


def moved(value, step):
    width = value.shape[-1]
    lane = lax.broadcasted_iota(jnp.int32, value.shape, value.ndim - 1)
    edge = 0 if step > 0 else width - 1
    return jnp.where(lane == edge, 0.0, pltpu.roll(value, step % width, value.ndim - 1))


def weight_kernel(at, w, a_hi, a_lo, b_hi, b_lo, token, turned):
    token[...] = jnp.zeros(token.shape, F32)
    side, chan = at[1], at[2]
    sign = 1 - 2 * side
    half = a_hi.shape[1] // 6
    full = 2 * half
    own = pl.ds(pl.multiple_of(chan * half, half), half)
    for first in range(3):
        for second in range(3):
            for third in range(3):
                tap = 9 * first + 3 * second + third
                turned[...] = w[tap].T
                fwd = halves(w[tap, own, :])
                back = halves(turned[own, :])
                fwd_at = 1 + (first - 1) * sign
                back_at = 1 - (first - 1) * sign
                for low in range(2):
                    up = low + second - 1
                    if up < 0 or up > 1:
                        continue
                    row = (low * 3 + third) * half
                    a_hi[fwd_at, row : row + half, up * full : up * full + full] = fwd[0]
                    a_lo[fwd_at, row : row + half, up * full : up * full + full] = fwd[1]
                    row = (up * 3 + 2 - third) * half
                    b_hi[back_at, row : row + half, low * full : low * full + full] = back[0]
                    b_lo[back_at, row : row + half, low * full : low * full + full] = back[1]


def put_slab(hi, lo, chan, own, other):
    half = own.shape[1]
    for z in range(2):
        for piece, place in ((own, chan), (other, 1 - chan)):
            rows = pl.ds(pl.multiple_of((2 * z + place) * half, half), half)
            hi[rows, :], lo[rows, :] = halves(piece[z])


def conv_kernel(places, at, *refs):
    *blocks, w_hi, w_lo, out, x_hi, x_lo = refs
    side, chan = at[1], at[2]
    half, width = out.shape[2:]
    for t in range(4):
        put_slab(
            x_hi.at[t],
            x_lo.at[t],
            chan,
            places[t](blocks, 0, side),
            places[t](blocks, 1, side),
        )
    for t in range(2):
        total = jnp.zeros((6 * half, width), F32)
        for d in range(3):
            total = total + dot3(w_hi[d], w_lo[d], x_hi[t + d], x_lo[t + d], NN)
        slab = side if t == 0 else 1 - side
        for z in range(2):
            low, mid, high = (
                total[(3 * z + c) * half : (3 * z + c + 1) * half, :] for c in range(3)
            )
            out[slab, z] = mid + moved(low, 1) + moved(high, -1)


def filter_kernel(at, own, own2, pair, pair2, edge, edge2, g_own, g_pair, _, *rest):
    count = len(rest) - 6
    outs = rest[:count]
    x_hi, x_lo, g_hi, g_lo, acc, flat = rest[count:]
    z_at, side, chan = at[0], at[1], at[2]
    half = own.shape[2]
    part = half // 2
    group = 6 * part
    slabs = (
        (own.at[side], own2.at[side]),
        (own.at[1 - side], own2.at[1 - side]),
        (pair.at[side], pair2.at[side]),
        (pair.at[1 - side], pair2.at[1 - side]),
        (edge.at[0], edge2.at[0]),
    )
    mine = pl.ds(pl.multiple_of(side * part, part), part)
    grads = (
        lambda z: g_own[side, z, mine, :],
        lambda z: g_own[1 - side, z, mine, :],
        lambda z: g_pair[side, z],
        lambda z: g_pair[1 - side, z],
        lambda z: edge[1, z, mine, :],
    )
    for t in range(5):
        put_slab(x_hi.at[t], x_lo.at[t], chan, *slabs[t])
        for z in range(2):
            value = grads[t](z)
            for c, shifted in enumerate((moved(value, -1), value, moved(value, 1))):
                row = t * group + (3 * z + c) * part
                g_hi[row : row + part, :], g_lo[row : row + part, :] = halves(shifted)

    def term(first, last, t):
        rows = slice(first * group, last * group)
        return dot3(g_hi[rows, :], g_lo[rows, :], x_hi[t], x_lo[t], NT)

    acc[...] = term(0, 3, 1) + term(1, 4, 2) + term(2, 5, 3)
    acc[group:, :] += term(0, 2, 0)
    acc[:group, :] += term(3, 4, 4)

    full = 2 * half
    tiles = flat.shape[0]
    place = 0
    for d in range(3):
        for b in range(3):
            for c in range(3):
                row = d * group + c * part
                lower = acc[row : row + part, :]
                upper = acc[row + 3 * part : row + 4 * part, :]
                if b == 0:
                    value = upper[:, :full]
                elif b == 1:
                    value = lower[:, :full] + upper[:, full:]
                else:
                    value = lower[:, full:]
                flat[place : place + part // 8] = value.reshape(part // 8, 8, full)
                place += part // 8
    if place < tiles:
        flat[place:] = jnp.zeros((tiles - place, 8, full), F32)
    each = tiles // count
    for k in range(count):
        outs[k][...] = flat[pl.ds(lax.rem(z_at + k, count) * each, each)]


def sum_kernel(scale, at, *refs):
    total = refs[0][...]
    for ref in refs[1:-1]:
        total = total + ref[...]
    refs[-1][...] = total * scale


def join_kernel(at, *refs):
    count = (len(refs) - 3) // 2
    mine, theirs = refs[:count], refs[count : 2 * count]
    out, flat, flat2 = refs[2 * count :]
    z_at, side = at[0], at[1]
    each = mine[0].shape[0]
    for k in range(count):
        here = pl.ds(lax.rem(z_at + count - k, count) * each, each)
        flat[here] = mine[k][...]
        flat2[here] = theirs[k][...]
    rows = out.shape[1] // 2
    for source, which in ((flat, side), (flat2, 1 - side)):
        for d, base in enumerate(((1 - which) * 18, 9, which * 18)):
            block = source[d * 9 * rows : (d + 1) * 9 * rows]
            out[pl.ds(base, 9), pl.ds(which * rows, rows)] = block.reshape(
                9, rows, 8, out.shape[3]
            )


def local(inputs, weights, out_grad):
    half, _, _, width = inputs.shape
    full = 2 * half
    ring = lax.axis_size("space")
    count = ring // 2
    here = lax.axis_index("space")
    z_at, side, chan = here // 2, here % 2, lax.axis_index("chan")
    at = jnp.stack([z_at, side, chan]).astype(jnp.int32)

    def swap_chan(value):
        return lax.ppermute(value, "chan", [(0, 1), (1, 0)])

    def swap_side(value):
        return lax.ppermute(value, "space", [(i, i ^ 1) for i in range(ring)])

    def shift(value, step):
        pairs = [(2 * z + y, 2 * ((z + step) % count) + y) for z in range(count) for y in range(2)]
        return lax.ppermute(value, "space", pairs)

    def outward(value):
        pairs = []
        for z in range(count):
            if z > 0:
                pairs.append((2 * z, 2 * z - 2))
            if z + 1 < count:
                pairs.append((2 * z + 1, 2 * z + 3))
        return lax.ppermute(value, "space", pairs)

    def slab(field, index):
        return lax.dynamic_index_in_dim(field, index, 0, keepdims=False)

    x_own = inputs.transpose(1, 2, 0, 3)
    x_pair = swap_side(x_own)
    x_own2 = swap_chan(x_own)
    g_own = out_grad.transpose(1, 2, 0, 3)
    g_pair = swap_side(lax.dynamic_slice_in_dim(g_own, (1 - side) * (half // 2), half // 2, 2))
    edge = outward(jnp.stack([slab(x_own, side), slab(g_own, side)]))
    g_own2 = swap_chan(g_own)

    w_taps = weights.transpose(1, 0, 2)
    block = jax.ShapeDtypeStruct((3, 6 * half, 2 * full), BF16)
    a_hi, a_lo, b_hi, b_lo, token = call(
        weight_kernel,
        [block] * 4 + [jax.ShapeDtypeStruct((8, full), F32)],
        1,
        [pltpu.VMEM((full, full), F32)],
    )(at, w_taps)
    x_pair, edge, token, _ = lax.optimization_barrier((x_pair, edge, token, g_pair))
    x_pair2 = swap_chan(x_pair)
    edge2 = swap_chan(edge)

    tiles = 27 * (half // 2) // 8
    each = -(-tiles // count)
    chunk = jax.ShapeDtypeStruct((each, 8, full), F32)
    group = 3 * half
    parts = call(
        filter_kernel,
        [chunk] * count,
        9,
        [
            pltpu.VMEM((5, 2 * full, width), BF16),
            pltpu.VMEM((5, 2 * full, width), BF16),
            pltpu.VMEM((5 * group, width), BF16),
            pltpu.VMEM((5 * group, width), BF16),
            pltpu.VMEM((3 * group, 2 * full), F32),
            pltpu.VMEM((each * count, 8, full), F32),
        ],
    )(at, x_own, x_own2, x_pair, x_pair2, edge, edge2, g_own, g_pair, token)

    late = swap_side(edge)
    next_g = swap_side(slab(g_own, 1 - side))
    got = [parts[0]] + [shift(parts[k], k) for k in range(1, count)]
    *got, late, next_g = lax.optimization_barrier((*got, late, next_g))
    late2 = swap_chan(late)
    next_g2 = swap_chan(next_g)

    def conv(places, *operands):
        return call(
            lambda *refs: conv_kernel(places, *refs),
            jax.ShapeDtypeStruct((2, 2, half, width), F32),
            len(operands),
            [pltpu.VMEM((4, 2 * full, width), BF16)] * 2,
        )(at, *operands)

    x_places = (
        lambda r, k, side: r[4 + k].at[0],
        lambda r, k, side: r[k].at[side],
        lambda r, k, side: r[k].at[1 - side],
        lambda r, k, side: r[2 + k].at[side],
    )
    g_places = (
        lambda r, k, side: r[2 + k].at[1],
        lambda r, k, side: r[k].at[side],
        lambda r, k, side: r[k].at[1 - side],
        lambda r, k, side: r[4 + k],
    )
    outputs = conv(x_places, x_own, x_own2, x_pair, x_pair2, late, late2, a_hi, a_lo)
    in_grad = conv(g_places, g_own, g_own2, late, late2, next_g, next_g2, b_hi, b_lo)
    outputs = outputs.transpose(2, 0, 1, 3)
    in_grad = in_grad.transpose(2, 0, 1, 3)
    cells = inputs.shape[1] * ring * inputs.shape[2] * width
    scale = float(1.0 / cells**0.5)
    shard = call(lambda *refs: sum_kernel(scale, *refs), chunk, count)(at, *got)
    mine = [shard] + [shift(shard, k) for k in range(1, count)]
    theirs = [swap_side(value) for value in mine]
    theirs[-1], outputs, in_grad = lax.optimization_barrier((theirs[-1], outputs, in_grad))
    joined = call(
        join_kernel,
        jax.ShapeDtypeStruct((27, half // 8, 8, full), F32),
        2 * count,
        [pltpu.VMEM((each * count, 8, full), F32)] * 2,
    )(at, *mine, *theirs)
    filter_grad = joined.reshape(27, half, full).transpose(1, 0, 2)
    return outputs, in_grad, filter_grad


def solution(mesh):
    in_specs = (
        P("chan", ("groups", "space"), None, None),
        P(),
        P("chan", ("groups", "space"), None, None),
    )
    out_specs = (
        P("chan", ("groups", "space"), None, None),
        P("chan", ("groups", "space"), None, None),
        P("chan", "groups", None),
    )
    return jax.shard_map(local, mesh=mesh, in_specs=in_specs, out_specs=out_specs, check_vma=False)
```

```python
import jax
import jax.numpy as jnp
from jax import lax
from jax.experimental import pallas as pl
from jax.experimental.pallas import tpu as pltpu
from jax.sharding import PartitionSpec as P

F32 = jnp.float32
BF16 = jnp.bfloat16
VMEM = pl.BlockSpec(memory_space=pltpu.VMEM)
SMEM = pl.BlockSpec(memory_space=pltpu.SMEM)
NN = (((1,), (0,)), ((), ()))
NT = (((1,), (1,)), ((), ()))


def call(body, out_shape, n_in, scratch=(), cost=None):
    return pl.pallas_call(
        body,
        out_shape=out_shape,
        in_specs=[SMEM] + [VMEM] * n_in,
        out_specs=jax.tree.map(lambda _: VMEM, out_shape),
        scratch_shapes=scratch,
        cost_estimate=cost,
        compiler_params=pltpu.CompilerParams(vmem_limit_bytes=40 << 20),
    )


def halves(value):
    high = value.astype(BF16)
    return high, (value - high.astype(F32)).astype(BF16)


def dot3(a_hi, a_lo, b_hi, b_lo, dims):
    def dot(a, b):
        return lax.dot_general(a, b, dims, preferred_element_type=F32)

    return dot(a_hi, b_hi) + (dot(a_hi, b_lo) + dot(a_lo, b_hi))


def moved(value, step):
    width = value.shape[-1]
    lane = lax.broadcasted_iota(jnp.int32, value.shape, value.ndim - 1)
    edge = 0 if step > 0 else width - 1
    return jnp.where(lane == edge, 0.0, pltpu.roll(value, step % width, value.ndim - 1))


def weight_kernel(at, w, a_hi, a_lo, b_hi, b_lo, token, turned):
    token[...] = jnp.zeros(token.shape, F32)
    side, chan = at[1], at[2]
    sign = 1 - 2 * side
    half = a_hi.shape[1] // 6
    full = 2 * half
    own = pl.ds(pl.multiple_of(chan * half, half), half)
    for first in range(3):
        for second in range(3):
            for third in range(3):
                tap = 9 * first + 3 * second + third
                turned[...] = w[tap].T
                fwd = halves(w[tap, own, :])
                back = halves(turned[own, :])
                fwd_at = 1 + (first - 1) * sign
                back_at = 1 - (first - 1) * sign
                for low in range(2):
                    up = low + second - 1
                    if up < 0 or up > 1:
                        continue
                    row = (low * 3 + third) * half
                    a_hi[fwd_at, row : row + half, up * full : up * full + full] = fwd[0]
                    a_lo[fwd_at, row : row + half, up * full : up * full + full] = fwd[1]
                    row = (up * 3 + 2 - third) * half
                    b_hi[back_at, row : row + half, low * full : low * full + full] = back[0]
                    b_lo[back_at, row : row + half, low * full : low * full + full] = back[1]


def put_slab(hi, lo, chan, own, other):
    half = own.shape[1]
    for z in range(2):
        for piece, place in ((own, chan), (other, 1 - chan)):
            rows = pl.ds(pl.multiple_of((2 * z + place) * half, half), half)
            hi[rows, :], lo[rows, :] = halves(piece[z])


def conv_kernel(places, at, *refs):
    *blocks, w_hi, w_lo, out, x_hi, x_lo = refs
    side, chan = at[1], at[2]
    half, width = out.shape[2:]
    for t in range(4):
        put_slab(
            x_hi.at[t],
            x_lo.at[t],
            chan,
            places[t](blocks, 0, side),
            places[t](blocks, 1, side),
        )
    for t in range(2):
        total = jnp.zeros((6 * half, width), F32)
        for d in range(3):
            total = total + dot3(w_hi[d], w_lo[d], x_hi[t + d], x_lo[t + d], NN)
        slab = side if t == 0 else 1 - side
        for z in range(2):
            low, mid, high = (
                total[(3 * z + c) * half : (3 * z + c + 1) * half, :] for c in range(3)
            )
            out[slab, z] = mid + moved(low, 1) + moved(high, -1)


def filter_kernel(at, own, own2, pair, pair2, edge, edge2, g_own, g_pair, _, *rest):
    count = len(rest) - 6
    outs = rest[:count]
    x_hi, x_lo, g_hi, g_lo, acc, flat = rest[count:]
    z_at, side, chan = at[0], at[1], at[2]
    half = own.shape[2]
    part = half // 2
    group = 6 * part
    slabs = (
        (own.at[side], own2.at[side]),
        (own.at[1 - side], own2.at[1 - side]),
        (pair.at[side], pair2.at[side]),
        (pair.at[1 - side], pair2.at[1 - side]),
        (edge.at[0], edge2.at[0]),
    )
    mine = pl.ds(pl.multiple_of(side * part, part), part)
    grads = (
        lambda z: g_own[side, z, mine, :],
        lambda z: g_own[1 - side, z, mine, :],
        lambda z: g_pair[side, z],
        lambda z: g_pair[1 - side, z],
        lambda z: edge[1, z, mine, :],
    )
    for t in range(5):
        put_slab(x_hi.at[t], x_lo.at[t], chan, *slabs[t])
        for z in range(2):
            value = grads[t](z)
            for c, shifted in enumerate((moved(value, -1), value, moved(value, 1))):
                row = t * group + (3 * z + c) * part
                g_hi[row : row + part, :], g_lo[row : row + part, :] = halves(shifted)

    def term(first, last, t):
        rows = slice(first * group, last * group)
        return dot3(g_hi[rows, :], g_lo[rows, :], x_hi[t], x_lo[t], NT)

    acc[...] = term(0, 3, 1) + term(1, 4, 2) + term(2, 5, 3)
    acc[group:, :] += term(0, 2, 0)
    acc[:group, :] += term(3, 4, 4)

    full = 2 * half
    tiles = flat.shape[0]
    place = 0
    for d in range(3):
        for b in range(3):
            for c in range(3):
                row = d * group + c * part
                lower = acc[row : row + part, :]
                upper = acc[row + 3 * part : row + 4 * part, :]
                if b == 0:
                    value = upper[:, :full]
                elif b == 1:
                    value = lower[:, :full] + upper[:, full:]
                else:
                    value = lower[:, full:]
                flat[place : place + part // 8] = value.reshape(part // 8, 8, full)
                place += part // 8
    if place < tiles:
        flat[place:] = jnp.zeros((tiles - place, 8, full), F32)
    each = tiles // count
    for k in range(count):
        outs[k][...] = flat[pl.ds(lax.rem(z_at + k, count) * each, each)]


def sum_kernel(scale, at, *refs):
    total = refs[0][...]
    for ref in refs[1:-1]:
        total = total + ref[...]
    refs[-1][...] = total * scale


def join_kernel(at, *refs):
    count = (len(refs) - 3) // 2
    mine, theirs = refs[:count], refs[count : 2 * count]
    out, flat, flat2 = refs[2 * count :]
    z_at, side = at[0], at[1]
    each = mine[0].shape[0]
    for k in range(count):
        here = pl.ds(lax.rem(z_at + count - k, count) * each, each)
        flat[here] = mine[k][...]
        flat2[here] = theirs[k][...]
    rows = out.shape[1] // 2
    for source, which in ((flat, side), (flat2, 1 - side)):
        for d, base in enumerate(((1 - which) * 18, 9, which * 18)):
            block = source[d * 9 * rows : (d + 1) * 9 * rows]
            out[pl.ds(base, 9), pl.ds(which * rows, rows)] = block.reshape(
                9, rows, 8, out.shape[3]
            )


def local(inputs, weights, out_grad):
    half, _, _, width = inputs.shape
    full = 2 * half
    ring = lax.axis_size("space")
    count = ring // 2
    here = lax.axis_index("space")
    z_at, side, chan = here // 2, here % 2, lax.axis_index("chan")
    at = jnp.stack([z_at, side, chan]).astype(jnp.int32)

    def swap_chan(value):
        return lax.ppermute(value, "chan", [(0, 1), (1, 0)])

    def swap_side(value):
        return lax.ppermute(value, "space", [(i, i ^ 1) for i in range(ring)])

    def shift(value, step):
        pairs = [(2 * z + y, 2 * ((z + step) % count) + y) for z in range(count) for y in range(2)]
        return lax.ppermute(value, "space", pairs)

    def outward(value):
        pairs = []
        for z in range(count):
            if z > 0:
                pairs.append((2 * z, 2 * z - 2))
            if z + 1 < count:
                pairs.append((2 * z + 1, 2 * z + 3))
        return lax.ppermute(value, "space", pairs)

    def slab(field, index):
        return lax.dynamic_index_in_dim(field, index, 0, keepdims=False)

    x_own = inputs.transpose(1, 2, 0, 3)
    x_pair = swap_side(x_own)
    x_own2 = swap_chan(x_own)
    g_own = out_grad.transpose(1, 2, 0, 3)
    g_pair = swap_side(lax.dynamic_slice_in_dim(g_own, (1 - side) * (half // 2), half // 2, 2))
    edge = outward(jnp.stack([slab(x_own, side), slab(g_own, side)]))
    g_own2 = swap_chan(g_own)

    w_taps = weights.transpose(1, 0, 2)
    block = jax.ShapeDtypeStruct((3, 6 * half, 2 * full), BF16)
    a_hi, a_lo, b_hi, b_lo, token = call(
        weight_kernel,
        [block] * 4 + [jax.ShapeDtypeStruct((8, full), F32)],
        1,
        [pltpu.VMEM((full, full), F32)],
    )(at, w_taps)
    x_pair, edge, token, _ = lax.optimization_barrier((x_pair, edge, token, g_pair))
    x_pair2 = swap_chan(x_pair)
    edge2 = swap_chan(edge)

    tiles = 27 * (half // 2) // 8
    each = -(-tiles // count)
    chunk = jax.ShapeDtypeStruct((each, 8, full), F32)
    group = 3 * half
    parts = call(
        filter_kernel,
        [chunk] * count,
        9,
        [
            pltpu.VMEM((5, 2 * full, width), BF16),
            pltpu.VMEM((5, 2 * full, width), BF16),
            pltpu.VMEM((5 * group, width), BF16),
            pltpu.VMEM((5 * group, width), BF16),
            pltpu.VMEM((3 * group, 2 * full), F32),
            pltpu.VMEM((each * count, 8, full), F32),
        ],
    )(at, x_own, x_own2, x_pair, x_pair2, edge, edge2, g_own, g_pair, token)

    late = swap_side(edge)
    next_g = swap_side(slab(g_own, 1 - side))
    got = [parts[0]] + [shift(parts[k], k) for k in range(1, count)]
    *got, late, next_g = lax.optimization_barrier((*got, late, next_g))
    late2 = swap_chan(late)
    next_g2 = swap_chan(next_g)

    def conv(places, *operands):
        return call(
            lambda *refs: conv_kernel(places, *refs),
            jax.ShapeDtypeStruct((2, 2, half, width), F32),
            len(operands),
            [pltpu.VMEM((4, 2 * full, width), BF16)] * 2,
        )(at, *operands)

    x_places = (
        lambda r, k, side: r[4 + k].at[0],
        lambda r, k, side: r[k].at[side],
        lambda r, k, side: r[k].at[1 - side],
        lambda r, k, side: r[2 + k].at[side],
    )
    g_places = (
        lambda r, k, side: r[2 + k].at[1],
        lambda r, k, side: r[k].at[side],
        lambda r, k, side: r[k].at[1 - side],
        lambda r, k, side: r[4 + k],
    )
    outputs = conv(x_places, x_own, x_own2, x_pair, x_pair2, late, late2, a_hi, a_lo)
    in_grad = conv(g_places, g_own, g_own2, late, late2, next_g, next_g2, b_hi, b_lo)
    outputs = outputs.transpose(2, 0, 1, 3)
    in_grad = in_grad.transpose(2, 0, 1, 3)
    cells = inputs.shape[1] * ring * inputs.shape[2] * width
    scale = float(1.0 / cells**0.5)
    shard = call(lambda *refs: sum_kernel(scale, *refs), chunk, count)(at, *got)
    mine = [shard] + [shift(shard, k) for k in range(1, count)]
    theirs = [swap_side(shard)]
    mine[1], outputs, in_grad, theirs[0] = lax.optimization_barrier(
        (mine[1], outputs, in_grad, theirs[0])
    )
    theirs += [swap_side(value) for value in mine[1:]]
    joined = call(
        join_kernel,
        jax.ShapeDtypeStruct((27, half // 8, 8, full), F32),
        2 * count,
        [pltpu.VMEM((each * count, 8, full), F32)] * 2,
    )(at, *mine, *theirs)
    filter_grad = joined.reshape(27, half, full).transpose(1, 0, 2)
    return outputs, in_grad, filter_grad


def solution(mesh):
    in_specs = (
        P("chan", ("groups", "space"), None, None),
        P(),
        P("chan", ("groups", "space"), None, None),
    )
    out_specs = (
        P("chan", ("groups", "space"), None, None),
        P("chan", ("groups", "space"), None, None),
        P("chan", "groups", None),
    )
    return jax.shard_map(local, mesh=mesh, in_specs=in_specs, out_specs=out_specs, check_vma=False)
```

```python
import jax
import jax.numpy as jnp
from jax import lax
from jax.experimental import pallas as pl
from jax.experimental.pallas import tpu as pltpu
from jax.sharding import PartitionSpec as P

F32 = jnp.float32
BF16 = jnp.bfloat16
VMEM = pl.BlockSpec(memory_space=pltpu.VMEM)
SMEM = pl.BlockSpec(memory_space=pltpu.SMEM)
NN = (((1,), (0,)), ((), ()))
NT = (((1,), (1,)), ((), ()))


def call(body, out_shape, n_in, scratch=(), cost=None):
    return pl.pallas_call(
        body,
        out_shape=out_shape,
        in_specs=[SMEM] + [VMEM] * n_in,
        out_specs=jax.tree.map(lambda _: VMEM, out_shape),
        scratch_shapes=scratch,
        cost_estimate=cost,
        compiler_params=pltpu.CompilerParams(vmem_limit_bytes=40 << 20),
    )


def halves(value):
    high = value.astype(BF16)
    return high, (value - high.astype(F32)).astype(BF16)


def dot3(a_hi, a_lo, b_hi, b_lo, dims):
    def dot(a, b):
        return lax.dot_general(a, b, dims, preferred_element_type=F32)

    return dot(a_hi, b_hi) + (dot(a_hi, b_lo) + dot(a_lo, b_hi))


def moved(value, step):
    width = value.shape[-1]
    lane = lax.broadcasted_iota(jnp.int32, value.shape, value.ndim - 1)
    edge = 0 if step > 0 else width - 1
    return jnp.where(lane == edge, 0.0, pltpu.roll(value, step % width, value.ndim - 1))


def weight_kernel(at, w, a_hi, a_lo, b_hi, b_lo, token, turned):
    token[...] = jnp.zeros(token.shape, F32)
    side, chan = at[1], at[2]
    sign = 1 - 2 * side
    half = a_hi.shape[1] // 6
    full = 2 * half
    own = pl.ds(pl.multiple_of(chan * half, half), half)
    for first in range(3):
        for second in range(3):
            for third in range(3):
                tap = 9 * first + 3 * second + third
                turned[...] = w[tap].T
                fwd = halves(w[tap, own, :])
                back = halves(turned[own, :])
                fwd_at = 1 + (first - 1) * sign
                back_at = 1 - (first - 1) * sign
                for low in range(2):
                    up = low + second - 1
                    if up < 0 or up > 1:
                        continue
                    row = (low * 3 + third) * half
                    a_hi[fwd_at, row : row + half, up * full : up * full + full] = fwd[0]
                    a_lo[fwd_at, row : row + half, up * full : up * full + full] = fwd[1]
                    row = (up * 3 + 2 - third) * half
                    b_hi[back_at, row : row + half, low * full : low * full + full] = back[0]
                    b_lo[back_at, row : row + half, low * full : low * full + full] = back[1]


def put_pieces(hi, lo, pieces):
    depth = hi.shape[0] // 2
    for piece, first in pieces:
        count = piece.shape[1]
        for z in range(2):
            rows = pl.ds(pl.multiple_of(z * depth + first, count), count)
            hi[rows, :], lo[rows, :] = halves(piece[z])


def put_slab(hi, lo, chan, own, other):
    half = own.shape[1]
    put_pieces(hi, lo, ((own, chan * half), (other, (1 - chan) * half)))


def conv_kernel(places, at, *refs):
    *blocks, w_hi, w_lo, out, x_hi, x_lo = refs
    side, chan = at[1], at[2]
    half, width = out.shape[2:]
    for t in range(4):
        put_pieces(x_hi.at[t], x_lo.at[t], places[t](blocks, side, chan))
    for t in range(2):
        total = jnp.zeros((6 * half, width), F32)
        for d in range(3):
            total = total + dot3(w_hi[d], w_lo[d], x_hi[t + d], x_lo[t + d], NN)
        slab = side if t == 0 else 1 - side
        for z in range(2):
            low, mid, high = (
                total[(3 * z + c) * half : (3 * z + c + 1) * half, :] for c in range(3)
            )
            out[slab, z] = mid + moved(low, 1) + moved(high, -1)


def put_grad(hi, lo, load, part):
    for z in range(2):
        value = load(z)
        for c, shifted in enumerate((moved(value, -1), value, moved(value, 1))):
            row = (3 * z + c) * part
            hi[row : row + part, :], lo[row : row + part, :] = halves(shifted)


def own_kernel(at, own, own2, g_own, _, acc, x1_hi, x1_lo, g1_hi, g1_lo, token, x_hi, x_lo, g_hi, g_lo):
    token[...] = jnp.zeros(token.shape, F32)
    side, chan = at[1], at[2]
    part = own.shape[2] // 2
    group = 6 * part
    mine = pl.ds(pl.multiple_of(side * part, part), part)
    for t, slab in enumerate((side, 1 - side)):
        put_slab(x_hi.at[t], x_lo.at[t], chan, own.at[slab], own2.at[slab])
        rows = pl.ds(t * group, group)
        put_grad(g_hi.at[rows], g_lo.at[rows], lambda z: g_own[slab, z, mine, :], part)
    x1_hi[...] = x_hi[1]
    x1_lo[...] = x_lo[1]
    g1_hi[...] = g_hi[group:, :]
    g1_lo[...] = g_lo[group:, :]
    later = dot3(g_hi[...], g_lo[...], x_hi[0], x_lo[0], NT)
    early = dot3(g_hi[...], g_lo[...], x_hi[1], x_lo[1], NT)
    acc[:group, :] = early[:group, :]
    acc[group : 2 * group, :] = early[group:, :] + later[:group, :]
    acc[2 * group :, :] = later[group:, :]


def filter_kernel(at, acc, x1_hi, x1_lo, g1_hi, g1_lo, pair, pair2, edge, edge2, g_pair, _, *rest):
    count = len(rest) - 6
    outs = rest[:count]
    x_hi, x_lo, g_hi, g_lo, sums, flat = rest[count:]
    z_at, side, chan = at[0], at[1], at[2]
    half = pair.shape[2]
    part = half // 2
    group = 6 * part
    slabs = (
        (pair.at[side], pair2.at[side]),
        (pair.at[1 - side], pair2.at[1 - side]),
        (edge.at[0], edge2.at[0]),
    )
    mine = pl.ds(pl.multiple_of(side * part, part), part)
    grads = (
        lambda z: g_pair[side, z],
        lambda z: g_pair[1 - side, z],
        lambda z: edge[1, z, mine, :],
    )
    g_hi[:group, :] = g1_hi[...]
    g_lo[:group, :] = g1_lo[...]
    for t in range(3):
        put_slab(x_hi.at[t], x_lo.at[t], chan, *slabs[t])
        rows = pl.ds((t + 1) * group, group)
        put_grad(g_hi.at[rows], g_lo.at[rows], grads[t], part)

    def term(first, last, hi, lo):
        rows = slice(first * group, last * group)
        return dot3(g_hi[rows, :], g_lo[rows, :], hi, lo, NT)

    sums[...] = acc[...] + term(0, 3, x_hi[0], x_lo[0]) + term(1, 4, x_hi[1], x_lo[1])
    sums[2 * group :, :] += term(1, 2, x1_hi[...], x1_lo[...])
    sums[:group, :] += term(2, 3, x_hi[2], x_lo[2])
    acc = sums

    full = 2 * half
    tiles = flat.shape[0]
    place = 0
    for d in range(3):
        for b in range(3):
            for c in range(3):
                row = d * group + c * part
                lower = acc[row : row + part, :]
                upper = acc[row + 3 * part : row + 4 * part, :]
                if b == 0:
                    value = upper[:, :full]
                elif b == 1:
                    value = lower[:, :full] + upper[:, full:]
                else:
                    value = lower[:, full:]
                flat[place : place + part // 8] = value.reshape(part // 8, 8, full)
                place += part // 8
    if place < tiles:
        flat[place:] = jnp.zeros((tiles - place, 8, full), F32)
    each = tiles // count
    for k in range(count):
        outs[k][...] = flat[pl.ds(lax.rem(z_at + k, count) * each, each)]


def sum_kernel(scale, at, *refs):
    total = refs[0][...]
    for ref in refs[1:-1]:
        total = total + ref[...]
    refs[-1][...] = total * scale


def join_kernel(at, *refs):
    count = (len(refs) - 3) // 2
    mine, theirs = refs[:count], refs[count : 2 * count]
    out, flat, flat2 = refs[2 * count :]
    z_at, side = at[0], at[1]
    each = mine[0].shape[0]
    for k in range(count):
        here = pl.ds(lax.rem(z_at + count - k, count) * each, each)
        flat[here] = mine[k][...]
        flat2[here] = theirs[k][...]
    rows = out.shape[1] // 2
    for source, which in ((flat, side), (flat2, 1 - side)):
        for d, base in enumerate(((1 - which) * 18, 9, which * 18)):
            block = source[d * 9 * rows : (d + 1) * 9 * rows]
            out[pl.ds(base, 9), pl.ds(which * rows, rows)] = block.reshape(
                9, rows, 8, out.shape[3]
            )


def local(inputs, weights, out_grad):
    half, _, _, width = inputs.shape
    full = 2 * half
    ring = lax.axis_size("space")
    count = ring // 2
    here = lax.axis_index("space")
    z_at, side, chan = here // 2, here % 2, lax.axis_index("chan")
    at = jnp.stack([z_at, side, chan]).astype(jnp.int32)

    def swap_chan(value):
        return lax.ppermute(value, "chan", [(0, 1), (1, 0)])

    def swap_side(value):
        return lax.ppermute(value, "space", [(i, i ^ 1) for i in range(ring)])

    def shift(value, step):
        pairs = [(2 * z + y, 2 * ((z + step) % count) + y) for z in range(count) for y in range(2)]
        return lax.ppermute(value, "space", pairs)

    def outward(value):
        pairs = []
        for z in range(count):
            if z > 0:
                pairs.append((2 * z, 2 * z - 2))
            if z + 1 < count:
                pairs.append((2 * z + 1, 2 * z + 3))
        return lax.ppermute(value, "space", pairs)

    def slab(field, index):
        return lax.dynamic_index_in_dim(field, index, 0, keepdims=False)

    x_own = inputs.transpose(1, 2, 0, 3)
    x_pair = swap_side(x_own)
    x_own2 = swap_chan(x_own)
    g_own = out_grad.transpose(1, 2, 0, 3)
    g_theirs = lax.dynamic_slice_in_dim(g_own, (1 - side) * (half // 2), half // 2, 2)
    g_ours = lax.dynamic_slice_in_dim(g_own, side * (half // 2), half // 2, 2)
    g_ours = lax.dynamic_slice_in_dim(g_ours, 1 - side, 1, 0)
    g_pair = swap_side(jnp.concatenate([g_theirs, g_ours]))
    edge = outward(jnp.stack([slab(x_own, side), slab(g_own, side)]))
    g_own2 = swap_chan(g_own)

    w_taps = weights.transpose(1, 0, 2)
    block = jax.ShapeDtypeStruct((3, 6 * half, 2 * full), BF16)
    a_hi, a_lo, b_hi, b_lo, token = call(
        weight_kernel,
        [block] * 4 + [jax.ShapeDtypeStruct((8, full), F32)],
        1,
        [pltpu.VMEM((full, full), F32)],
    )(at, w_taps)
    group = 3 * half
    slab_half = jax.ShapeDtypeStruct((2 * full, width), BF16)
    grad_half = jax.ShapeDtypeStruct((group, width), BF16)
    *inner, done = call(
        own_kernel,
        [jax.ShapeDtypeStruct((3 * group, 2 * full), F32)]
        + [slab_half] * 2
        + [grad_half] * 2
        + [jax.ShapeDtypeStruct((8, full), F32)],
        4,
        [pltpu.VMEM((2, 2 * full, width), BF16)] * 2 + [pltpu.VMEM((2 * group, width), BF16)] * 2,
    )(at, x_own, x_own2, g_own, token)
    x_pair, done = lax.optimization_barrier((x_pair, done))
    edge, _ = lax.optimization_barrier((edge, g_pair))
    x_pair2 = swap_chan(x_pair)
    edge2 = swap_chan(edge)

    tiles = 27 * (half // 2) // 8
    each = -(-tiles // count)
    chunk = jax.ShapeDtypeStruct((each, 8, full), F32)
    parts = call(
        filter_kernel,
        [chunk] * count,
        11,
        [pltpu.VMEM((3, 2 * full, width), BF16)] * 2
        + [pltpu.VMEM((4 * group, width), BF16)] * 2
        + [pltpu.VMEM((3 * group, 2 * full), F32), pltpu.VMEM((each * count, 8, full), F32)],
    )(at, *inner, x_pair, x_pair2, edge, edge2, g_pair, done)

    late = swap_side(edge)
    got = [parts[0]] + [shift(parts[k], k) for k in range(1, count)]
    *got, late = lax.optimization_barrier((*got, late))
    late2 = swap_chan(late)
    g_pair2 = swap_chan(g_pair)

    def conv(places, *operands):
        return call(
            lambda *refs: conv_kernel(places, *refs),
            jax.ShapeDtypeStruct((2, 2, half, width), F32),
            len(operands),
            [pltpu.VMEM((4, 2 * full, width), BF16)] * 2,
        )(at, *operands)

    def both(own, other, chan):
        return ((own, chan * half), (other, (1 - chan) * half))

    def quarters(r, side, chan):
        part = half // 2
        return tuple(
            (block, core * half + which * part)
            for pair, core in ((r[4], chan), (r[5], 1 - chan))
            for block, which in ((pair.at[side], side), (pair.at[2], 1 - side))
        )

    x_places = (
        lambda r, side, chan: both(r[4].at[0], r[5].at[0], chan),
        lambda r, side, chan: both(r[0].at[side], r[1].at[side], chan),
        lambda r, side, chan: both(r[0].at[1 - side], r[1].at[1 - side], chan),
        lambda r, side, chan: both(r[2].at[side], r[3].at[side], chan),
    )
    g_places = (
        lambda r, side, chan: both(r[2].at[1], r[3].at[1], chan),
        lambda r, side, chan: both(r[0].at[side], r[1].at[side], chan),
        lambda r, side, chan: both(r[0].at[1 - side], r[1].at[1 - side], chan),
        quarters,
    )
    outputs = conv(x_places, x_own, x_own2, x_pair, x_pair2, late, late2, a_hi, a_lo)
    in_grad = conv(g_places, g_own, g_own2, late, late2, g_pair, g_pair2, b_hi, b_lo)
    outputs = outputs.transpose(2, 0, 1, 3)
    in_grad = in_grad.transpose(2, 0, 1, 3)
    cells = inputs.shape[1] * ring * inputs.shape[2] * width
    scale = float(1.0 / cells**0.5)
    shard = call(lambda *refs: sum_kernel(scale, *refs), chunk, count)(at, *got)
    mine = [shard] + [shift(shard, k) for k in range(1, count)]
    theirs = [swap_side(shard)]
    mine[1], outputs, in_grad, theirs[0] = lax.optimization_barrier(
        (mine[1], outputs, in_grad, theirs[0])
    )
    theirs += [swap_side(value) for value in mine[1:]]
    joined = call(
        join_kernel,
        jax.ShapeDtypeStruct((27, half // 8, 8, full), F32),
        2 * count,
        [pltpu.VMEM((each * count, 8, full), F32)] * 2,
    )(at, *mine, *theirs)
    filter_grad = joined.reshape(27, half, full).transpose(1, 0, 2)
    return outputs, in_grad, filter_grad


def solution(mesh):
    in_specs = (
        P("chan", ("groups", "space"), None, None),
        P(),
        P("chan", ("groups", "space"), None, None),
    )
    out_specs = (
        P("chan", ("groups", "space"), None, None),
        P("chan", ("groups", "space"), None, None),
        P("chan", "groups", None),
    )
    return jax.shard_map(local, mesh=mesh, in_specs=in_specs, out_specs=out_specs, check_vma=False)
```

```python
import jax
import jax.numpy as jnp
from jax import lax
from jax.experimental import pallas as pl
from jax.experimental.pallas import tpu as pltpu
from jax.sharding import PartitionSpec as P

F32 = jnp.float32
BF16 = jnp.bfloat16
VMEM = pl.BlockSpec(memory_space=pltpu.VMEM)
SMEM = pl.BlockSpec(memory_space=pltpu.SMEM)
NN = (((1,), (0,)), ((), ()))
NT = (((1,), (1,)), ((), ()))


def call(body, out_shape, n_in, scratch=(), cost=None):
    return pl.pallas_call(
        body,
        out_shape=out_shape,
        in_specs=[SMEM] + [VMEM] * n_in,
        out_specs=jax.tree.map(lambda _: VMEM, out_shape),
        scratch_shapes=scratch,
        cost_estimate=cost,
        compiler_params=pltpu.CompilerParams(vmem_limit_bytes=40 << 20),
    )


def halves(value):
    high = value.astype(BF16)
    return high, (value - high.astype(F32)).astype(BF16)


def dot3(a_hi, a_lo, b_hi, b_lo, dims):
    def dot(a, b):
        return lax.dot_general(a, b, dims, preferred_element_type=F32)

    return dot(a_hi, b_hi) + (dot(a_hi, b_lo) + dot(a_lo, b_hi))


def moved(value, step):
    width = value.shape[-1]
    lane = lax.broadcasted_iota(jnp.int32, value.shape, value.ndim - 1)
    edge = 0 if step > 0 else width - 1
    return jnp.where(lane == edge, 0.0, pltpu.roll(value, step % width, value.ndim - 1))


def weight_kernel(at, w, a_hi, a_lo, b_hi, b_lo, token, turned):
    token[...] = jnp.zeros(token.shape, F32)
    side, chan = at[1], at[2]
    sign = 1 - 2 * side
    half = a_hi.shape[1] // 6
    full = 2 * half
    own = pl.ds(pl.multiple_of(chan * half, half), half)
    for first in range(3):
        for second in range(3):
            for third in range(3):
                tap = 9 * first + 3 * second + third
                turned[...] = w[tap].T
                fwd = halves(w[tap, own, :])
                back = halves(turned[own, :])
                fwd_at = 1 + (first - 1) * sign
                back_at = 1 - (first - 1) * sign
                for low in range(2):
                    up = low + second - 1
                    if up < 0 or up > 1:
                        continue
                    row = (low * 3 + third) * half
                    a_hi[fwd_at, row : row + half, up * full : up * full + full] = fwd[0]
                    a_lo[fwd_at, row : row + half, up * full : up * full + full] = fwd[1]
                    row = (up * 3 + 2 - third) * half
                    b_hi[back_at, row : row + half, low * full : low * full + full] = back[0]
                    b_lo[back_at, row : row + half, low * full : low * full + full] = back[1]


def put_pieces(hi, lo, pieces):
    depth = hi.shape[0] // 2
    for piece, first in pieces:
        count = piece.shape[1]
        for z in range(2):
            rows = pl.ds(pl.multiple_of(z * depth + first, count), count)
            hi[rows, :], lo[rows, :] = halves(piece[z])


def put_slab(hi, lo, chan, own, other):
    half = own.shape[1]
    put_pieces(hi, lo, ((own, chan * half), (other, (1 - chan) * half)))


def conv_kernel(places, at, *refs):
    *blocks, w_hi, w_lo, out, x_hi, x_lo = refs
    side, chan = at[1], at[2]
    half, width = out.shape[2:]
    for t in range(4):
        put_pieces(x_hi.at[t], x_lo.at[t], places[t](blocks, side, chan))
    for t in range(2):
        total = jnp.zeros((6 * half, width), F32)
        for d in range(3):
            total = total + dot3(w_hi[d], w_lo[d], x_hi[t + d], x_lo[t + d], NN)
        slab = side if t == 0 else 1 - side
        for z in range(2):
            low, mid, high = (
                total[(3 * z + c) * half : (3 * z + c + 1) * half, :] for c in range(3)
            )
            out[slab, z] = mid + moved(low, 1) + moved(high, -1)


def put_grad(hi, lo, load, part):
    for z in range(2):
        value = load(z)
        for c, shifted in enumerate((moved(value, -1), value, moved(value, 1))):
            row = (3 * z + c) * part
            hi[row : row + part, :], lo[row : row + part, :] = halves(shifted)


def own_kernel(at, own, own2, g_own, _, acc, x1_hi, x1_lo, g1_hi, g1_lo, token, x_hi, x_lo, g_hi, g_lo):
    token[...] = jnp.zeros(token.shape, F32)
    side, chan = at[1], at[2]
    part = own.shape[2] // 2
    group = 6 * part
    mine = pl.ds(pl.multiple_of(side * part, part), part)
    for t, slab in enumerate((side, 1 - side)):
        put_slab(x_hi.at[t], x_lo.at[t], chan, own.at[slab], own2.at[slab])
        rows = pl.ds(t * group, group)
        put_grad(g_hi.at[rows], g_lo.at[rows], lambda z: g_own[slab, z, mine, :], part)
    x1_hi[...] = x_hi[1]
    x1_lo[...] = x_lo[1]
    g1_hi[...] = g_hi[group:, :]
    g1_lo[...] = g_lo[group:, :]
    later = dot3(g_hi[...], g_lo[...], x_hi[0], x_lo[0], NT)
    early = dot3(g_hi[...], g_lo[...], x_hi[1], x_lo[1], NT)
    acc[:group, :] = early[:group, :]
    acc[group : 2 * group, :] = early[group:, :] + later[:group, :]
    acc[2 * group :, :] = later[group:, :]


def filter_kernel(at, acc, x1_hi, x1_lo, g1_hi, g1_lo, pair, pair2, edge, edge2, g_pair, _, *rest):
    count = len(rest) - 6
    outs = rest[:count]
    x_hi, x_lo, g_hi, g_lo, sums, flat = rest[count:]
    z_at, side, chan = at[0], at[1], at[2]
    half = pair.shape[2]
    part = half // 2
    group = 6 * part
    slabs = (
        (pair.at[side], pair2.at[side]),
        (pair.at[1 - side], pair2.at[1 - side]),
        (edge.at[0], edge2.at[0]),
    )
    mine = pl.ds(pl.multiple_of(side * part, part), part)
    grads = (
        lambda z: g_pair[side, z],
        lambda z: g_pair[1 - side, z],
        lambda z: edge[1, z, mine, :],
    )
    g_hi[:group, :] = g1_hi[...]
    g_lo[:group, :] = g1_lo[...]
    for t in range(3):
        put_slab(x_hi.at[t], x_lo.at[t], chan, *slabs[t])
        rows = pl.ds((t + 1) * group, group)
        put_grad(g_hi.at[rows], g_lo.at[rows], grads[t], part)

    def term(first, last, hi, lo):
        rows = slice(first * group, last * group)
        return dot3(g_hi[rows, :], g_lo[rows, :], hi, lo, NT)

    sums[...] = acc[...] + term(0, 3, x_hi[0], x_lo[0]) + term(1, 4, x_hi[1], x_lo[1])
    sums[2 * group :, :] += term(1, 2, x1_hi[...], x1_lo[...])
    sums[:group, :] += term(2, 3, x_hi[2], x_lo[2])
    acc = sums

    full = 2 * half
    tiles = flat.shape[0]
    place = 0
    for d in range(3):
        for b in range(3):
            for c in range(3):
                row = d * group + c * part
                lower = acc[row : row + part, :]
                upper = acc[row + 3 * part : row + 4 * part, :]
                if b == 0:
                    value = upper[:, :full]
                elif b == 1:
                    value = lower[:, :full] + upper[:, full:]
                else:
                    value = lower[:, full:]
                flat[place : place + part // 8] = value.reshape(part // 8, 8, full)
                place += part // 8
    if place < tiles:
        flat[place:] = jnp.zeros((tiles - place, 8, full), F32)
    each = tiles // count
    for k in range(count):
        outs[k][...] = flat[pl.ds(lax.rem(z_at + k, count) * each, each)]


def sum_kernel(scale, at, *refs):
    total = refs[0][...]
    for ref in refs[1:-1]:
        total = total + ref[...]
    refs[-1][...] = total * scale


def join_kernel(at, *refs):
    count = (len(refs) - 3) // 2
    mine, theirs = refs[:count], refs[count : 2 * count]
    out, flat, flat2 = refs[2 * count :]
    z_at, side = at[0], at[1]
    each = mine[0].shape[0]
    for k in range(count):
        here = pl.ds(lax.rem(z_at + count - k, count) * each, each)
        flat[here] = mine[k][...]
        flat2[here] = theirs[k][...]
    rows = out.shape[1] // 2
    for source, which in ((flat, side), (flat2, 1 - side)):
        for d, base in enumerate(((1 - which) * 18, 9, which * 18)):
            block = source[d * 9 * rows : (d + 1) * 9 * rows]
            out[pl.ds(base, 9), pl.ds(which * rows, rows)] = block.reshape(
                9, rows, 8, out.shape[3]
            )


def local(inputs, weights, out_grad):
    half, _, _, width = inputs.shape
    full = 2 * half
    ring = lax.axis_size("space")
    count = ring // 2
    here = lax.axis_index("space")
    z_at, side, chan = here // 2, here % 2, lax.axis_index("chan")
    at = jnp.stack([z_at, side, chan]).astype(jnp.int32)

    def swap_chan(value):
        return lax.ppermute(value, "chan", [(0, 1), (1, 0)])

    def swap_side(value):
        return lax.ppermute(value, "space", [(i, i ^ 1) for i in range(ring)])

    def shift(value, step):
        pairs = [(2 * z + y, 2 * ((z + step) % count) + y) for z in range(count) for y in range(2)]
        return lax.ppermute(value, "space", pairs)

    def outward(value):
        pairs = []
        for z in range(count):
            if z > 0:
                pairs.append((2 * z, 2 * z - 2))
            if z + 1 < count:
                pairs.append((2 * z + 1, 2 * z + 3))
        return lax.ppermute(value, "space", pairs)

    def slab(field, index):
        return lax.dynamic_index_in_dim(field, index, 0, keepdims=False)

    x_own = inputs.transpose(1, 2, 0, 3)
    x_pair = swap_side(x_own)
    g_own = out_grad.transpose(1, 2, 0, 3)
    x_next, g_own = lax.optimization_barrier((x_own, g_own))
    x_own2 = swap_chan(x_next)
    g_theirs = lax.dynamic_slice_in_dim(g_own, (1 - side) * (half // 2), half // 2, 2)
    g_ours = lax.dynamic_slice_in_dim(g_own, side * (half // 2), half // 2, 2)
    g_ours = lax.dynamic_slice_in_dim(g_ours, 1 - side, 1, 0)
    g_pair = swap_side(jnp.concatenate([g_theirs, g_ours]))
    edge = outward(jnp.stack([slab(x_own, side), slab(g_own, side)]))
    g_own2 = swap_chan(g_own)

    w_taps = weights.transpose(1, 0, 2)
    block = jax.ShapeDtypeStruct((3, 6 * half, 2 * full), BF16)
    a_hi, a_lo, b_hi, b_lo, token = call(
        weight_kernel,
        [block] * 4 + [jax.ShapeDtypeStruct((8, full), F32)],
        1,
        [pltpu.VMEM((full, full), F32)],
    )(at, w_taps)
    group = 3 * half
    slab_half = jax.ShapeDtypeStruct((2 * full, width), BF16)
    grad_half = jax.ShapeDtypeStruct((group, width), BF16)
    *inner, done = call(
        own_kernel,
        [jax.ShapeDtypeStruct((3 * group, 2 * full), F32)]
        + [slab_half] * 2
        + [grad_half] * 2
        + [jax.ShapeDtypeStruct((8, full), F32)],
        4,
        [pltpu.VMEM((2, 2 * full, width), BF16)] * 2 + [pltpu.VMEM((2 * group, width), BF16)] * 2,
    )(at, x_own, x_own2, g_own, token)
    x_pair, done = lax.optimization_barrier((x_pair, done))
    edge, _ = lax.optimization_barrier((edge, g_pair))
    x_pair2 = swap_chan(x_pair)
    edge2 = swap_chan(edge)

    tiles = 27 * (half // 2) // 8
    each = -(-tiles // count)
    chunk = jax.ShapeDtypeStruct((each, 8, full), F32)
    parts = call(
        filter_kernel,
        [chunk] * count,
        11,
        [pltpu.VMEM((3, 2 * full, width), BF16)] * 2
        + [pltpu.VMEM((4 * group, width), BF16)] * 2
        + [pltpu.VMEM((3 * group, 2 * full), F32), pltpu.VMEM((each * count, 8, full), F32)],
    )(at, *inner, x_pair, x_pair2, edge, edge2, g_pair, done)

    late = swap_side(edge)
    got = [parts[0]] + [shift(parts[k], k) for k in range(1, count)]
    *got, late = lax.optimization_barrier((*got, late))
    late2 = swap_chan(late)
    g_pair2 = swap_chan(g_pair)

    def conv(places, *operands):
        return call(
            lambda *refs: conv_kernel(places, *refs),
            jax.ShapeDtypeStruct((2, 2, half, width), F32),
            len(operands),
            [pltpu.VMEM((4, 2 * full, width), BF16)] * 2,
        )(at, *operands)

    def both(own, other, chan):
        return ((own, chan * half), (other, (1 - chan) * half))

    def quarters(r, side, chan):
        part = half // 2
        return tuple(
            (block, core * half + which * part)
            for pair, core in ((r[4], chan), (r[5], 1 - chan))
            for block, which in ((pair.at[side], side), (pair.at[2], 1 - side))
        )

    x_places = (
        lambda r, side, chan: both(r[4].at[0], r[5].at[0], chan),
        lambda r, side, chan: both(r[0].at[side], r[1].at[side], chan),
        lambda r, side, chan: both(r[0].at[1 - side], r[1].at[1 - side], chan),
        lambda r, side, chan: both(r[2].at[side], r[3].at[side], chan),
    )
    g_places = (
        lambda r, side, chan: both(r[2].at[1], r[3].at[1], chan),
        lambda r, side, chan: both(r[0].at[side], r[1].at[side], chan),
        lambda r, side, chan: both(r[0].at[1 - side], r[1].at[1 - side], chan),
        quarters,
    )
    outputs = conv(x_places, x_own, x_own2, x_pair, x_pair2, late, late2, a_hi, a_lo)
    in_grad = conv(g_places, g_own, g_own2, late, late2, g_pair, g_pair2, b_hi, b_lo)
    outputs = outputs.transpose(2, 0, 1, 3)
    in_grad = in_grad.transpose(2, 0, 1, 3)
    cells = inputs.shape[1] * ring * inputs.shape[2] * width
    scale = float(1.0 / cells**0.5)
    shard = call(lambda *refs: sum_kernel(scale, *refs), chunk, count)(at, *got)
    mine = [shard] + [shift(shard, k) for k in range(1, count)]
    theirs = [swap_side(shard)]
    mine[1], outputs, in_grad, theirs[0] = lax.optimization_barrier(
        (mine[1], outputs, in_grad, theirs[0])
    )
    theirs += [swap_side(value) for value in mine[1:]]
    joined = call(
        join_kernel,
        jax.ShapeDtypeStruct((27, half // 8, 8, full), F32),
        2 * count,
        [pltpu.VMEM((each * count, 8, full), F32)] * 2,
    )(at, *mine, *theirs)
    filter_grad = joined.reshape(27, half, full).transpose(1, 0, 2)
    return outputs, in_grad, filter_grad


def solution(mesh):
    in_specs = (
        P("chan", ("groups", "space"), None, None),
        P(),
        P("chan", ("groups", "space"), None, None),
    )
    out_specs = (
        P("chan", ("groups", "space"), None, None),
        P("chan", ("groups", "space"), None, None),
        P("chan", "groups", None),
    )
    return jax.shard_map(local, mesh=mesh, in_specs=in_specs, out_specs=out_specs, check_vma=False)
```

```python
import jax
import jax.numpy as jnp
from jax import lax
from jax.experimental import pallas as pl
from jax.experimental.pallas import tpu as pltpu
from jax.sharding import PartitionSpec as P

F32 = jnp.float32
BF16 = jnp.bfloat16
VMEM = pl.BlockSpec(memory_space=pltpu.VMEM)
SMEM = pl.BlockSpec(memory_space=pltpu.SMEM)
NN = (((1,), (0,)), ((), ()))
NT = (((1,), (1,)), ((), ()))


def call(body, out_shape, n_in, scratch=(), cost=None):
    return pl.pallas_call(
        body,
        out_shape=out_shape,
        in_specs=[SMEM] + [VMEM] * n_in,
        out_specs=jax.tree.map(lambda _: VMEM, out_shape),
        scratch_shapes=scratch,
        cost_estimate=cost,
        compiler_params=pltpu.CompilerParams(vmem_limit_bytes=40 << 20),
    )


def halves(value):
    high = value.astype(BF16)
    return high, (value - high.astype(F32)).astype(BF16)


def dot3(a_hi, a_lo, b_hi, b_lo, dims):
    def dot(a, b):
        return lax.dot_general(a, b, dims, preferred_element_type=F32)

    return dot(a_hi, b_hi) + (dot(a_hi, b_lo) + dot(a_lo, b_hi))


def moved(value, step):
    width = value.shape[-1]
    lane = lax.broadcasted_iota(jnp.int32, value.shape, value.ndim - 1)
    edge = 0 if step > 0 else width - 1
    return jnp.where(lane == edge, 0.0, pltpu.roll(value, step % width, value.ndim - 1))


def weight_kernel(at, w, a_hi, a_lo, b_hi, b_lo, token, turned):
    token[...] = jnp.zeros(token.shape, F32)
    side, chan = at[1], at[2]
    sign = 1 - 2 * side
    half = a_hi.shape[1] // 6
    full = 2 * half
    own = pl.ds(pl.multiple_of(chan * half, half), half)
    for first in range(3):
        for second in range(3):
            for third in range(3):
                tap = 9 * first + 3 * second + third
                turned[...] = w[tap].T
                fwd = halves(w[tap, own, :])
                back = halves(turned[own, :])
                fwd_at = 1 + (first - 1) * sign
                back_at = 1 - (first - 1) * sign
                for low in range(2):
                    up = low + second - 1
                    if up < 0 or up > 1:
                        continue
                    row = (low * 3 + third) * half
                    a_hi[fwd_at, row : row + half, up * full : up * full + full] = fwd[0]
                    a_lo[fwd_at, row : row + half, up * full : up * full + full] = fwd[1]
                    row = (up * 3 + 2 - third) * half
                    b_hi[back_at, row : row + half, low * full : low * full + full] = back[0]
                    b_lo[back_at, row : row + half, low * full : low * full + full] = back[1]


def put_pieces(hi, lo, pieces):
    depth = hi.shape[0] // 2
    for piece, first in pieces:
        count = piece.shape[1]
        for z in range(2):
            rows = pl.ds(pl.multiple_of(z * depth + first, count), count)
            hi[rows, :], lo[rows, :] = halves(piece[z])


def put_slab(hi, lo, chan, own, other):
    half = own.shape[1]
    put_pieces(hi, lo, ((own, chan * half), (other, (1 - chan) * half)))


def conv_kernel(places, at, *refs):
    *blocks, w_hi, w_lo, out, x_hi, x_lo = refs
    side, chan = at[1], at[2]
    half, width = out.shape[2:]
    for t in range(4):
        put_pieces(x_hi.at[t], x_lo.at[t], places[t](blocks, side, chan))
    for t in range(2):
        total = jnp.zeros((6 * half, width), F32)
        for d in range(3):
            total = total + dot3(w_hi[d], w_lo[d], x_hi[t + d], x_lo[t + d], NN)
        slab = side if t == 0 else 1 - side
        for z in range(2):
            low, mid, high = (
                total[(3 * z + c) * half : (3 * z + c + 1) * half, :] for c in range(3)
            )
            out[slab, z] = mid + moved(low, 1) + moved(high, -1)


def put_grad(hi, lo, load, part):
    for z in range(2):
        value = load(z)
        for c, shifted in enumerate((moved(value, -1), value, moved(value, 1))):
            row = (3 * z + c) * part
            hi[row : row + part, :], lo[row : row + part, :] = halves(shifted)


def own_kernel(at, own, own2, g_own, _, acc, x1_hi, x1_lo, g1_hi, g1_lo, token, x_hi, x_lo, g_hi, g_lo):
    token[...] = jnp.zeros(token.shape, F32)
    side, chan = at[1], at[2]
    part = own.shape[2] // 2
    group = 6 * part
    mine = pl.ds(pl.multiple_of(side * part, part), part)
    for t, slab in enumerate((side, 1 - side)):
        put_slab(x_hi.at[t], x_lo.at[t], chan, own.at[slab], own2.at[slab])
        rows = pl.ds(t * group, group)
        put_grad(g_hi.at[rows], g_lo.at[rows], lambda z: g_own[slab, z, mine, :], part)
    x1_hi[...] = x_hi[1]
    x1_lo[...] = x_lo[1]
    g1_hi[...] = g_hi[group:, :]
    g1_lo[...] = g_lo[group:, :]
    later = dot3(g_hi[...], g_lo[...], x_hi[0], x_lo[0], NT)
    early = dot3(g_hi[...], g_lo[...], x_hi[1], x_lo[1], NT)
    acc[:group, :] = early[:group, :]
    acc[group : 2 * group, :] = early[group:, :] + later[:group, :]
    acc[2 * group :, :] = later[group:, :]


def filter_kernel(at, acc, x1_hi, x1_lo, g1_hi, g1_lo, pair, pair2, edge, edge2, g_pair, _, *rest):
    count = len(rest) - 6
    outs = rest[:count]
    x_hi, x_lo, g_hi, g_lo, sums, flat = rest[count:]
    z_at, side, chan = at[0], at[1], at[2]
    half = pair.shape[2]
    part = half // 2
    group = 6 * part
    slabs = (
        (pair.at[side], pair2.at[side]),
        (pair.at[1 - side], pair2.at[1 - side]),
        (edge.at[0], edge2.at[0]),
    )
    mine = pl.ds(pl.multiple_of(side * part, part), part)
    grads = (
        lambda z: g_pair[side, z],
        lambda z: g_pair[1 - side, z],
        lambda z: edge[1, z, mine, :],
    )
    g_hi[:group, :] = g1_hi[...]
    g_lo[:group, :] = g1_lo[...]
    for t in range(3):
        put_slab(x_hi.at[t], x_lo.at[t], chan, *slabs[t])
        rows = pl.ds((t + 1) * group, group)
        put_grad(g_hi.at[rows], g_lo.at[rows], grads[t], part)

    def term(first, last, hi, lo):
        rows = slice(first * group, last * group)
        return dot3(g_hi[rows, :], g_lo[rows, :], hi, lo, NT)

    sums[...] = acc[...] + term(0, 3, x_hi[0], x_lo[0]) + term(1, 4, x_hi[1], x_lo[1])
    sums[2 * group :, :] += term(1, 2, x1_hi[...], x1_lo[...])
    sums[:group, :] += term(2, 3, x_hi[2], x_lo[2])
    acc = sums

    full = 2 * half
    tiles = flat.shape[0]
    place = 0
    for d in range(3):
        for b in range(3):
            for c in range(3):
                row = d * group + c * part
                lower = acc[row : row + part, :]
                upper = acc[row + 3 * part : row + 4 * part, :]
                if b == 0:
                    value = upper[:, :full]
                elif b == 1:
                    value = lower[:, :full] + upper[:, full:]
                else:
                    value = lower[:, full:]
                flat[place : place + part // 8] = value.reshape(part // 8, 8, full)
                place += part // 8
    if place < tiles:
        flat[place:] = jnp.zeros((tiles - place, 8, full), F32)
    each = tiles // count
    for k in range(count):
        outs[k][...] = flat[pl.ds(lax.rem(z_at + k, count) * each, each)]


def sum_kernel(scale, at, *refs):
    total = refs[0][...]
    for ref in refs[1:-1]:
        total = total + ref[...]
    refs[-1][...] = total * scale


def join_kernel(at, *refs):
    count = (len(refs) - 3) // 2
    mine, theirs = refs[:count], refs[count : 2 * count]
    out, flat, flat2 = refs[2 * count :]
    z_at, side = at[0], at[1]
    each = mine[0].shape[0]
    for k in range(count):
        here = pl.ds(lax.rem(z_at + count - k, count) * each, each)
        flat[here] = mine[k][...]
        flat2[here] = theirs[k][...]
    rows = out.shape[1] // 2
    for source, which in ((flat, side), (flat2, 1 - side)):
        for d, base in enumerate(((1 - which) * 18, 9, which * 18)):
            block = source[d * 9 * rows : (d + 1) * 9 * rows]
            out[pl.ds(base, 9), pl.ds(which * rows, rows)] = block.reshape(
                9, rows, 8, out.shape[3]
            )


def local(inputs, weights, out_grad):
    half, _, _, width = inputs.shape
    full = 2 * half
    ring = lax.axis_size("space")
    count = ring // 2
    here = lax.axis_index("space")
    z_at, side, chan = here // 2, here % 2, lax.axis_index("chan")
    at = jnp.stack([z_at, side, chan]).astype(jnp.int32)

    def swap_chan(value):
        return lax.ppermute(value, "chan", [(0, 1), (1, 0)])

    def swap_side(value):
        return lax.ppermute(value, "space", [(i, i ^ 1) for i in range(ring)])

    def shift(value, step):
        pairs = [(2 * z + y, 2 * ((z + step) % count) + y) for z in range(count) for y in range(2)]
        return lax.ppermute(value, "space", pairs)

    def outward(value):
        pairs = []
        for z in range(count):
            if z > 0:
                pairs.append((2 * z, 2 * z - 2))
            if z + 1 < count:
                pairs.append((2 * z + 1, 2 * z + 3))
        return lax.ppermute(value, "space", pairs)

    def slab(field, index):
        return lax.dynamic_index_in_dim(field, index, 0, keepdims=False)

    x_own = inputs.transpose(1, 2, 0, 3)
    x_pair = swap_side(x_own)
    g_own = out_grad.transpose(1, 2, 0, 3)
    x_next, g_own = lax.optimization_barrier((x_own, g_own))
    x_own2 = swap_chan(x_next)
    g_theirs = lax.dynamic_slice_in_dim(g_own, (1 - side) * (half // 2), half // 2, 2)
    g_ours = lax.dynamic_slice_in_dim(g_own, side * (half // 2), half // 2, 2)
    g_ours = lax.dynamic_slice_in_dim(g_ours, 1 - side, 1, 0)
    g_pair = swap_side(jnp.concatenate([g_theirs, g_ours]))
    edge = outward(jnp.stack([slab(x_own, side), slab(g_own, side)]))
    g_own2 = swap_chan(g_own)

    w_taps = weights.transpose(1, 0, 2)
    block = jax.ShapeDtypeStruct((3, 6 * half, 2 * full), BF16)
    a_hi, a_lo, b_hi, b_lo, token = call(
        weight_kernel,
        [block] * 4 + [jax.ShapeDtypeStruct((8, full), F32)],
        1,
        [pltpu.VMEM((full, full), F32)],
    )(at, w_taps)
    group = 3 * half
    slab_half = jax.ShapeDtypeStruct((2 * full, width), BF16)
    grad_half = jax.ShapeDtypeStruct((group, width), BF16)
    *inner, done = call(
        own_kernel,
        [jax.ShapeDtypeStruct((3 * group, 2 * full), F32)]
        + [slab_half] * 2
        + [grad_half] * 2
        + [jax.ShapeDtypeStruct((8, full), F32)],
        4,
        [pltpu.VMEM((2, 2 * full, width), BF16)] * 2 + [pltpu.VMEM((2 * group, width), BF16)] * 2,
    )(at, x_own, x_own2, g_own, token)
    x_pair, done = lax.optimization_barrier((x_pair, done))
    edge, _ = lax.optimization_barrier((edge, g_pair))
    x_pair2 = swap_chan(x_pair)
    edge2 = swap_chan(edge)

    tiles = 27 * (half // 2) // 8
    each = -(-tiles // count)
    chunk = jax.ShapeDtypeStruct((each, 8, full), F32)
    parts = call(
        filter_kernel,
        [chunk] * count,
        11,
        [pltpu.VMEM((3, 2 * full, width), BF16)] * 2
        + [pltpu.VMEM((4 * group, width), BF16)] * 2
        + [pltpu.VMEM((3 * group, 2 * full), F32), pltpu.VMEM((each * count, 8, full), F32)],
    )(at, *inner, x_pair, x_pair2, edge, edge2, g_pair, done)

    late = swap_side(edge)
    got = [parts[0]] + [shift(parts[k], k) for k in range(1, count)]
    *got, late = lax.optimization_barrier((*got, late))
    late2 = swap_chan(late)

    def conv(places, *operands):
        return call(
            lambda *refs: conv_kernel(places, *refs),
            jax.ShapeDtypeStruct((2, 2, half, width), F32),
            len(operands),
            [pltpu.VMEM((4, 2 * full, width), BF16)] * 2,
        )(at, *operands)

    def both(own, other, chan):
        return ((own, chan * half), (other, (1 - chan) * half))

    def quarters(r, side, chan):
        part = half // 2
        return tuple(
            (block, core * half + which * part)
            for pair, core in ((r[4], chan), (r[5], 1 - chan))
            for block, which in ((pair.at[side], side), (pair.at[2], 1 - side))
        )

    x_places = (
        lambda r, side, chan: both(r[4].at[0], r[5].at[0], chan),
        lambda r, side, chan: both(r[0].at[side], r[1].at[side], chan),
        lambda r, side, chan: both(r[0].at[1 - side], r[1].at[1 - side], chan),
        lambda r, side, chan: both(r[2].at[side], r[3].at[side], chan),
    )
    g_places = (
        lambda r, side, chan: both(r[2].at[1], r[3].at[1], chan),
        lambda r, side, chan: both(r[0].at[side], r[1].at[side], chan),
        lambda r, side, chan: both(r[0].at[1 - side], r[1].at[1 - side], chan),
        quarters,
    )
    outputs = conv(x_places, x_own, x_own2, x_pair, x_pair2, late, late2, a_hi, a_lo)
    outputs = outputs.transpose(2, 0, 1, 3)
    cells = inputs.shape[1] * ring * inputs.shape[2] * width
    scale = float(1.0 / cells**0.5)
    shard = call(lambda *refs: sum_kernel(scale, *refs), chunk, count)(at, *got)
    shard, g_pair = lax.optimization_barrier((shard, g_pair))
    g_pair2 = swap_chan(g_pair)
    in_grad = conv(g_places, g_own, g_own2, late, late2, g_pair, g_pair2, b_hi, b_lo)
    in_grad = in_grad.transpose(2, 0, 1, 3)
    mine = [shard] + [shift(shard, k) for k in range(1, count)]
    theirs = [swap_side(shard)]
    mine[1], outputs, in_grad, theirs[0] = lax.optimization_barrier(
        (mine[1], outputs, in_grad, theirs[0])
    )
    theirs += [swap_side(value) for value in mine[1:]]
    joined = call(
        join_kernel,
        jax.ShapeDtypeStruct((27, half // 8, 8, full), F32),
        2 * count,
        [pltpu.VMEM((each * count, 8, full), F32)] * 2,
    )(at, *mine, *theirs)
    filter_grad = joined.reshape(27, half, full).transpose(1, 0, 2)
    return outputs, in_grad, filter_grad


def solution(mesh):
    in_specs = (
        P("chan", ("groups", "space"), None, None),
        P(),
        P("chan", ("groups", "space"), None, None),
    )
    out_specs = (
        P("chan", ("groups", "space"), None, None),
        P("chan", ("groups", "space"), None, None),
        P("chan", "groups", None),
    )
    return jax.shard_map(local, mesh=mesh, in_specs=in_specs, out_specs=out_specs, check_vma=False)
```

```python
import jax
import jax.numpy as jnp
from jax import lax
from jax.experimental import pallas as pl
from jax.experimental.pallas import tpu as pltpu
from jax.sharding import PartitionSpec as P

F32 = jnp.float32
BF16 = jnp.bfloat16
VMEM = pl.BlockSpec(memory_space=pltpu.VMEM)
SMEM = pl.BlockSpec(memory_space=pltpu.SMEM)
NN = (((1,), (0,)), ((), ()))
NT = (((1,), (1,)), ((), ()))


def call(body, out_shape, n_in, scratch=(), cost=None):
    return pl.pallas_call(
        body,
        out_shape=out_shape,
        in_specs=[SMEM] + [VMEM] * n_in,
        out_specs=jax.tree.map(lambda _: VMEM, out_shape),
        scratch_shapes=scratch,
        cost_estimate=cost,
        compiler_params=pltpu.CompilerParams(vmem_limit_bytes=40 << 20),
    )


def halves(value):
    high = value.astype(BF16)
    return high, (value - high.astype(F32)).astype(BF16)


def dot3(a_hi, a_lo, b_hi, b_lo, dims):
    def dot(a, b):
        return lax.dot_general(a, b, dims, preferred_element_type=F32)

    return dot(a_hi, b_hi) + (dot(a_hi, b_lo) + dot(a_lo, b_hi))


def moved(value, step):
    width = value.shape[-1]
    lane = lax.broadcasted_iota(jnp.int32, value.shape, value.ndim - 1)
    edge = 0 if step > 0 else width - 1
    return jnp.where(lane == edge, 0.0, pltpu.roll(value, step % width, value.ndim - 1))


def weight_kernel(at, w, a_hi, a_lo, b_hi, b_lo, token, turned):
    token[...] = jnp.zeros(token.shape, F32)
    side, chan = at[1], at[2]
    sign = 1 - 2 * side
    half = a_hi.shape[1] // 6
    full = 2 * half
    own = pl.ds(pl.multiple_of(chan * half, half), half)
    for first in range(3):
        for second in range(3):
            for third in range(3):
                tap = 9 * first + 3 * second + third
                turned[...] = w[tap].T
                fwd = halves(w[tap, own, :])
                back = halves(turned[own, :])
                fwd_at = 1 + (first - 1) * sign
                back_at = 1 - (first - 1) * sign
                for low in range(2):
                    up = low + second - 1
                    if up < 0 or up > 1:
                        continue
                    row = (low * 3 + third) * half
                    a_hi[fwd_at, row : row + half, up * full : up * full + full] = fwd[0]
                    a_lo[fwd_at, row : row + half, up * full : up * full + full] = fwd[1]
                    row = (up * 3 + 2 - third) * half
                    b_hi[back_at, row : row + half, low * full : low * full + full] = back[0]
                    b_lo[back_at, row : row + half, low * full : low * full + full] = back[1]


def put_pieces(hi, lo, pieces):
    depth = hi.shape[0] // 2
    for piece, first in pieces:
        count = piece.shape[1]
        for z in range(2):
            rows = pl.ds(pl.multiple_of(z * depth + first, count), count)
            hi[rows, :], lo[rows, :] = halves(piece[z])


def put_slab(hi, lo, chan, own, other):
    half = own.shape[1]
    put_pieces(hi, lo, ((own, chan * half), (other, (1 - chan) * half)))


def conv_kernel(places, at, *refs):
    *blocks, w_hi, w_lo, out, x_hi, x_lo = refs
    side, chan = at[1], at[2]
    half, width = out.shape[2:]
    for t in range(4):
        put_pieces(x_hi.at[t], x_lo.at[t], places[t](blocks, side, chan))
    for t in range(2):
        total = jnp.zeros((6 * half, width), F32)
        for d in range(3):
            total = total + dot3(w_hi[d], w_lo[d], x_hi[t + d], x_lo[t + d], NN)
        slab = side if t == 0 else 1 - side
        for z in range(2):
            low, mid, high = (
                total[(3 * z + c) * half : (3 * z + c + 1) * half, :] for c in range(3)
            )
            out[slab, z] = mid + moved(low, 1) + moved(high, -1)


def put_grad(hi, lo, load, part):
    for z in range(2):
        value = load(z)
        for c, shifted in enumerate((moved(value, -1), value, moved(value, 1))):
            row = (3 * z + c) * part
            hi[row : row + part, :], lo[row : row + part, :] = halves(shifted)


def own_kernel(at, own, own2, g_own, _, acc, x1_hi, x1_lo, g1_hi, g1_lo, token, x_hi, x_lo, g_hi, g_lo):
    token[...] = jnp.zeros(token.shape, F32)
    side, chan = at[1], at[2]
    part = own.shape[2] // 2
    group = 6 * part
    mine = pl.ds(pl.multiple_of(side * part, part), part)
    for t, slab in enumerate((side, 1 - side)):
        put_slab(x_hi.at[t], x_lo.at[t], chan, own.at[slab], own2.at[slab])
        rows = pl.ds(t * group, group)
        put_grad(g_hi.at[rows], g_lo.at[rows], lambda z: g_own[slab, z, mine, :], part)
    x1_hi[...] = x_hi[1]
    x1_lo[...] = x_lo[1]
    g1_hi[...] = g_hi[group:, :]
    g1_lo[...] = g_lo[group:, :]
    later = dot3(g_hi[...], g_lo[...], x_hi[0], x_lo[0], NT)
    early = dot3(g_hi[...], g_lo[...], x_hi[1], x_lo[1], NT)
    acc[:group, :] = early[:group, :]
    acc[group : 2 * group, :] = early[group:, :] + later[:group, :]
    acc[2 * group :, :] = later[group:, :]


def filter_kernel(at, acc, x1_hi, x1_lo, g1_hi, g1_lo, pair, pair2, edge, edge2, g_pair, _, *rest):
    count = len(rest) - 6
    outs = rest[:count]
    x_hi, x_lo, g_hi, g_lo, sums, flat = rest[count:]
    z_at, side, chan = at[0], at[1], at[2]
    half = pair.shape[2]
    part = half // 2
    group = 6 * part
    slabs = (
        (pair.at[side], pair2.at[side]),
        (pair.at[1 - side], pair2.at[1 - side]),
        (edge.at[0], edge2.at[0]),
    )
    mine = pl.ds(pl.multiple_of(side * part, part), part)
    grads = (
        lambda z: g_pair[side, z],
        lambda z: g_pair[1 - side, z],
        lambda z: edge[1, z, mine, :],
    )
    g_hi[:group, :] = g1_hi[...]
    g_lo[:group, :] = g1_lo[...]
    for t in range(3):
        put_slab(x_hi.at[t], x_lo.at[t], chan, *slabs[t])
        rows = pl.ds((t + 1) * group, group)
        put_grad(g_hi.at[rows], g_lo.at[rows], grads[t], part)

    def term(first, last, hi, lo):
        rows = slice(first * group, last * group)
        return dot3(g_hi[rows, :], g_lo[rows, :], hi, lo, NT)

    inner = term(0, 3, x_hi[0], x_lo[0]) + term(1, 4, x_hi[1], x_lo[1])
    first = term(2, 3, x_hi[2], x_lo[2])
    last = term(1, 2, x1_hi[...], x1_lo[...])
    sums[:group, :] = acc[:group, :] + inner[:group, :] + first
    sums[group : 2 * group, :] = acc[group : 2 * group, :] + inner[group : 2 * group, :]
    sums[2 * group :, :] = acc[2 * group :, :] + inner[2 * group :, :] + last
    acc = sums

    full = 2 * half
    tiles = flat.shape[0]
    place = 0
    for d in range(3):
        for b in range(3):
            for c in range(3):
                row = d * group + c * part
                lower = acc[row : row + part, :]
                upper = acc[row + 3 * part : row + 4 * part, :]
                if b == 0:
                    value = upper[:, :full]
                elif b == 1:
                    value = lower[:, :full] + upper[:, full:]
                else:
                    value = lower[:, full:]
                flat[place : place + part // 8] = value.reshape(part // 8, 8, full)
                place += part // 8
    if place < tiles:
        flat[place:] = jnp.zeros((tiles - place, 8, full), F32)
    each = tiles // count
    for k in range(count):
        outs[k][...] = flat[pl.ds(lax.rem(z_at + k, count) * each, each)]


def sum_kernel(scale, at, *refs):
    total = refs[0][...]
    for ref in refs[1:-1]:
        total = total + ref[...]
    refs[-1][...] = total * scale


def join_kernel(at, *refs):
    count = (len(refs) - 3) // 2
    mine, theirs = refs[:count], refs[count : 2 * count]
    out, flat, flat2 = refs[2 * count :]
    z_at, side = at[0], at[1]
    each = mine[0].shape[0]
    for k in range(count):
        here = pl.ds(lax.rem(z_at + count - k, count) * each, each)
        flat[here] = mine[k][...]
        flat2[here] = theirs[k][...]
    rows = out.shape[1] // 2
    for source, which in ((flat, side), (flat2, 1 - side)):
        for d, base in enumerate(((1 - which) * 18, 9, which * 18)):
            block = source[d * 9 * rows : (d + 1) * 9 * rows]
            out[pl.ds(base, 9), pl.ds(which * rows, rows)] = block.reshape(
                9, rows, 8, out.shape[3]
            )


def local(inputs, weights, out_grad):
    half, _, _, width = inputs.shape
    full = 2 * half
    ring = lax.axis_size("space")
    count = ring // 2
    here = lax.axis_index("space")
    z_at, side, chan = here // 2, here % 2, lax.axis_index("chan")
    at = jnp.stack([z_at, side, chan]).astype(jnp.int32)

    def swap_chan(value):
        return lax.ppermute(value, "chan", [(0, 1), (1, 0)])

    def swap_side(value):
        return lax.ppermute(value, "space", [(i, i ^ 1) for i in range(ring)])

    def shift(value, step):
        pairs = [(2 * z + y, 2 * ((z + step) % count) + y) for z in range(count) for y in range(2)]
        return lax.ppermute(value, "space", pairs)

    def outward(value):
        pairs = []
        for z in range(count):
            if z > 0:
                pairs.append((2 * z, 2 * z - 2))
            if z + 1 < count:
                pairs.append((2 * z + 1, 2 * z + 3))
        return lax.ppermute(value, "space", pairs)

    def slab(field, index):
        return lax.dynamic_index_in_dim(field, index, 0, keepdims=False)

    x_own = inputs.transpose(1, 2, 0, 3)
    x_pair = swap_side(x_own)
    g_own = out_grad.transpose(1, 2, 0, 3)
    x_next, g_own = lax.optimization_barrier((x_own, g_own))
    x_own2 = swap_chan(x_next)
    g_theirs = lax.dynamic_slice_in_dim(g_own, (1 - side) * (half // 2), half // 2, 2)
    g_ours = lax.dynamic_slice_in_dim(g_own, side * (half // 2), half // 2, 2)
    g_ours = lax.dynamic_slice_in_dim(g_ours, 1 - side, 1, 0)
    g_pair = swap_side(jnp.concatenate([g_theirs, g_ours]))
    edge = outward(jnp.stack([slab(x_own, side), slab(g_own, side)]))
    g_own2 = swap_chan(g_own)

    w_taps = weights.transpose(1, 0, 2)
    block = jax.ShapeDtypeStruct((3, 6 * half, 2 * full), BF16)
    a_hi, a_lo, b_hi, b_lo, token = call(
        weight_kernel,
        [block] * 4 + [jax.ShapeDtypeStruct((8, full), F32)],
        1,
        [pltpu.VMEM((full, full), F32)],
    )(at, w_taps)
    group = 3 * half
    slab_half = jax.ShapeDtypeStruct((2 * full, width), BF16)
    grad_half = jax.ShapeDtypeStruct((group, width), BF16)
    *inner, done = call(
        own_kernel,
        [jax.ShapeDtypeStruct((3 * group, 2 * full), F32)]
        + [slab_half] * 2
        + [grad_half] * 2
        + [jax.ShapeDtypeStruct((8, full), F32)],
        4,
        [pltpu.VMEM((2, 2 * full, width), BF16)] * 2 + [pltpu.VMEM((2 * group, width), BF16)] * 2,
    )(at, x_own, x_own2, g_own, token)
    x_pair, done = lax.optimization_barrier((x_pair, done))
    edge, _ = lax.optimization_barrier((edge, g_pair))
    x_pair2 = swap_chan(x_pair)
    edge2 = swap_chan(edge)

    tiles = 27 * (half // 2) // 8
    each = -(-tiles // count)
    chunk = jax.ShapeDtypeStruct((each, 8, full), F32)
    parts = call(
        filter_kernel,
        [chunk] * count,
        11,
        [pltpu.VMEM((3, 2 * full, width), BF16)] * 2
        + [pltpu.VMEM((4 * group, width), BF16)] * 2
        + [pltpu.VMEM((3 * group, 2 * full), F32), pltpu.VMEM((each * count, 8, full), F32)],
    )(at, *inner, x_pair, x_pair2, edge, edge2, g_pair, done)

    late = swap_side(edge)
    got = [parts[0]] + [shift(parts[k], k) for k in range(1, count)]
    *got, late = lax.optimization_barrier((*got, late))
    late2 = swap_chan(late)

    def conv(places, *operands):
        return call(
            lambda *refs: conv_kernel(places, *refs),
            jax.ShapeDtypeStruct((2, 2, half, width), F32),
            len(operands),
            [pltpu.VMEM((4, 2 * full, width), BF16)] * 2,
        )(at, *operands)

    def both(own, other, chan):
        return ((own, chan * half), (other, (1 - chan) * half))

    def quarters(r, side, chan):
        part = half // 2
        return tuple(
            (block, core * half + which * part)
            for pair, core in ((r[4], chan), (r[5], 1 - chan))
            for block, which in ((pair.at[side], side), (pair.at[2], 1 - side))
        )

    x_places = (
        lambda r, side, chan: both(r[4].at[0], r[5].at[0], chan),
        lambda r, side, chan: both(r[0].at[side], r[1].at[side], chan),
        lambda r, side, chan: both(r[0].at[1 - side], r[1].at[1 - side], chan),
        lambda r, side, chan: both(r[2].at[side], r[3].at[side], chan),
    )
    g_places = (
        lambda r, side, chan: both(r[2].at[1], r[3].at[1], chan),
        lambda r, side, chan: both(r[0].at[side], r[1].at[side], chan),
        lambda r, side, chan: both(r[0].at[1 - side], r[1].at[1 - side], chan),
        quarters,
    )
    outputs = conv(x_places, x_own, x_own2, x_pair, x_pair2, late, late2, a_hi, a_lo)
    outputs = outputs.transpose(2, 0, 1, 3)
    cells = inputs.shape[1] * ring * inputs.shape[2] * width
    scale = float(1.0 / cells**0.5)
    shard = call(lambda *refs: sum_kernel(scale, *refs), chunk, count)(at, *got)
    shard, g_pair = lax.optimization_barrier((shard, g_pair))
    g_pair2 = swap_chan(g_pair)
    in_grad = conv(g_places, g_own, g_own2, late, late2, g_pair, g_pair2, b_hi, b_lo)
    in_grad = in_grad.transpose(2, 0, 1, 3)
    mine = [shard] + [shift(shard, k) for k in range(1, count)]
    theirs = [swap_side(shard)]
    mine[1], outputs, in_grad, theirs[0] = lax.optimization_barrier(
        (mine[1], outputs, in_grad, theirs[0])
    )
    theirs += [swap_side(value) for value in mine[1:]]
    joined = call(
        join_kernel,
        jax.ShapeDtypeStruct((27, half // 8, 8, full), F32),
        2 * count,
        [pltpu.VMEM((each * count, 8, full), F32)] * 2,
    )(at, *mine, *theirs)
    filter_grad = joined.reshape(27, half, full).transpose(1, 0, 2)
    return outputs, in_grad, filter_grad


def solution(mesh):
    in_specs = (
        P("chan", ("groups", "space"), None, None),
        P(),
        P("chan", ("groups", "space"), None, None),
    )
    out_specs = (
        P("chan", ("groups", "space"), None, None),
        P("chan", ("groups", "space"), None, None),
        P("chan", "groups", None),
    )
    return jax.shard_map(local, mesh=mesh, in_specs=in_specs, out_specs=out_specs, check_vma=False)
```
